32 devices in a mesh: gy: 8 (over y, x, core), gz: 4 (over z).
Axes of the slice: x: 2, y: 2, z: 4, core: 2. Of those that a mesh axis runs over, the one named last changes fastest.
Arguments:
- volume: float32 [64, 128, 1024], P('gz', None, 'gy'), may hold values from -6 to 6
- contrast: float32 [128], replicated, may hold values from 0.1 to 1
Outputs:
- filtered: float32 [64, 128, 1024], P('gz', None, 'gy')
The draws below stay inside these ranges and needn't reach their ends.
All inputs are finite; a program needn't handle non-finite values.
Results may differ from the reference program's by a relative error of at most 0.0003.
Values sent between devices are 32-bit elements; how exact they have to be, the bound alone decides.
A program may use at most 192 MiB of HBM per device.

```python
import math
import jax
import jax.numpy as jnp
from jax import lax

NX = 128
STEPS = 2
NY = 1024
NZ = 64


def steps_of(rng, extent, split, least, largest):
    level = 1.0
    for dim, shards_of in split:
        heights = jax.random.uniform(jax.random.fold_in(jax.random.fold_in(rng, 6), dim), (shards_of,), jnp.float32, least / len(split), largest / len(split))
        level = level * jnp.repeat(jnp.exp(heights), extent[dim] // shards_of).reshape((-1,) + (1,) * (len(extent) - 1 - dim))
    return level


def scatter_about(key, dims, deviation, limit, shards=(), kind=jnp.bfloat16):
    loudness = steps_of(key, dims, shards, -0.22, 0.18) if shards else 1.0
    drawn = jax.random.normal(key, dims, jnp.float32) * deviation * loudness
    return jnp.minimum(jnp.maximum(drawn, -limit), limit).astype(kind)


def setup_inputs(seed: int = 0) -> dict:
    streams_of = jax.random.split(jax.random.key(seed), 3)
    return {
        "volume": scatter_about(streams_of[0], (NZ, NX, NY), 1.0, 6.0, ((0, 4), (2, 8)), jnp.float32),
        "contrast": jnp.clip(jnp.exp(jax.random.uniform(streams_of[1], (NX,), jnp.float32, math.log(0.1), math.log(1.0))), 0.1, 1.0),
    }


kernel_taps = (0.05448868, 0.24420134, 0.40261995, 0.24420134, 0.05448868)
half_scale = 600.0


def slice_axis(array, start, count, axis, stride=1):
    return lax.slice_in_dim(array, start, start + stride * (count - 1) + 1, stride, axis)


def reduce_solve(lower, diagonal, upper, right, axis):
    length = right.shape[axis]
    if length == 1:
        return right / diagonal
    count_even = (length + 1) // 2
    count_odd = length // 2
    evens = [slice_axis(array, 0, count_even, axis, 2) for array in (lower, diagonal, upper, right)]
    odds = [slice_axis(array, 1, count_odd, axis, 2) for array in (lower, diagonal, upper, right)]
    before = [slice_axis(array, 0, count_odd, axis) for array in evens]
    zero_one = jnp.zeros_like(slice_axis(evens[0], 0, 1, axis))
    padding = [zero_one, zero_one + 1.0, zero_one, zero_one]
    after = [slice_axis(jnp.concatenate([array, extra], axis), 1, count_odd, axis) for array, extra in zip(evens, padding)]
    factor_before = -odds[0] / before[1]
    factor_after = -odds[2] / after[1]
    new_lower = factor_before * before[0]
    new_diag = odds[1] + factor_before * before[2] + factor_after * after[0]
    new_upper = factor_after * after[2]
    new_right = odds[3] + factor_before * before[3] + factor_after * after[3]
    solved_odd = reduce_solve(new_lower, new_diag, new_upper, new_right, axis)
    zero_row = jnp.zeros_like(slice_axis(solved_odd, 0, 1, axis))
    extra_rows = [zero_row] * (count_even - count_odd)
    padded_odd = jnp.concatenate([zero_row, solved_odd] + extra_rows, axis)
    left_value = slice_axis(padded_odd, 0, count_even, axis)
    right_value = slice_axis(padded_odd, 1, count_even, axis)
    solved_even = (evens[3] - evens[0] * left_value - evens[2] * right_value) / evens[1]
    odd_full = jnp.concatenate([solved_odd] + extra_rows, axis)
    paired = jnp.stack([solved_even, odd_full], axis=axis + 1)
    shape = right.shape[:axis] + (2 * count_even,) + right.shape[axis + 1:]
    return slice_axis(paired.reshape(shape), 0, length, axis)


def line_solve(upper, right, axis):
    length = upper.shape[axis]
    lower = jnp.concatenate([jnp.zeros_like(slice_axis(upper, 0, 1, axis)), slice_axis(upper, 0, length - 1, axis)], axis)
    diagonal = 1.0 + lower + upper
    return reduce_solve(-lower, diagonal, -upper, right, axis)


def smooth_axis(padded, axis):
    count = padded.shape[axis] - 4
    total = kernel_taps[0] * slice_axis(padded, 0, count, axis)
    for offset in range(1, 5):
        total = total + kernel_taps[offset] * slice_axis(padded, offset, count, axis)
    return total


def face_upper(diffusivity, axis):
    length = diffusivity.shape[axis]
    inner = (slice_axis(diffusivity, 0, length - 1, axis) + slice_axis(diffusivity, 1, length - 1, axis)) * half_scale
    return jnp.concatenate([inner, jnp.zeros_like(slice_axis(diffusivity, 0, 1, axis))], axis)


def reference(volume, contrast):
    current = volume
    for repeat in range(STEPS):
        blurred = jnp.pad(current, 2)
        blurred = smooth_axis(blurred, 0)
        blurred = smooth_axis(blurred, 2)
        blurred = smooth_axis(blurred, 1)
        extended = jnp.pad(blurred, 1)
        grad_z = (extended[2:, 1:-1, 1:-1] - extended[:-2, 1:-1, 1:-1]) * 0.5
        grad_y = (extended[1:-1, 1:-1, 2:] - extended[1:-1, 1:-1, :-2]) * 0.5
        grad_x = (extended[1:-1, 2:, 1:-1] - extended[1:-1, :-2, 1:-1]) * 0.5
        square = grad_x * grad_x + grad_y * grad_y + grad_z * grad_z
        diffusivity = 1.0 / (1.0 + square / (contrast * contrast)[None, :, None])
        solved_x = line_solve(face_upper(diffusivity, 1), current, 1)
        solved_y = line_solve(face_upper(diffusivity, 2), current, 2)
        solved_z = line_solve(face_upper(diffusivity, 0), current, 0)
        current = (solved_x + solved_y + solved_z) / 3.0
    return current
```

```python
import functools

import jax
import jax.numpy as jnp
from jax import lax
from jax.experimental import pallas as pl
from jax.experimental.pallas import tpu as pltpu
from jax.sharding import PartitionSpec as P

STEPS = 2
TAPS = (0.05448868, 0.24420134, 0.40261995, 0.24420134, 0.05448868)
SCALE = 600.0
MESH = pl.DeviceIdType.MESH
DIRECTIONS = [(dy, dz) for dz in (-1, 1, 0) for dy in (0, -1, 1) if (dy, dz) != (0, 0)]
PAD = 8
HALO = 4
CHUNK = 32
STENCIL_ROWS = 48


def merge(left, right):
    ea, ra, eb, rb, g, f = left
    ea2, ra2, eb2, rb2, g2, f2 = right
    s1 = 1.0 / (eb + g + f)
    wg, wf, q1 = g * s1, f * s1, rb * s1
    ea = ea + wg * eb
    ra = ra + wg * rb
    ea2 = ea2 + wf * eb
    ra2 = ra2 + wf * rb
    g1 = wf * g
    s2 = 1.0 / (ea2 + g1 + g2)
    vg, vf, q2 = g1 * s2, g2 * s2, ra2 * s2
    joined = (ea + vg * ea2, ra + vg * ra2, eb2 + vf * ea2, rb2 + vf * ra2, vf * g1, f2)
    return joined, (wg, wf, q1, vg, vf, q2)


def unmerge(weights, va, vb):
    wg, wf, q1, vg, vf, q2 = weights
    inner_right = vg * va + vf * vb + q2
    inner_left = wg * va + wf * inner_right + q1
    return inner_left, inner_right


def solve_pair(ea, ra, eb, rb, g):
    s = 1.0 / (ea + g)
    w = g * s
    vb = (rb + w * ra) / (eb + w * ea)
    return w * vb + ra * s, vb


def kernel(ny, nz, rounds, vol, con, out, c_ref, t_ref, b_ref, d_ref, dt_ref, wx_ref, wy_ref, wz_ref, vx_ref, vy_ref,
           vz_ref, zr_ref, zi_ref, zsend, zbuf, zvsend, zv, ysend, yrecv,
           halo_s, halo_r, zs, zrs, zvs, zvr, ys, yr):
    depth, nx, cols = vol.shape
    rows = cols + 2 * PAD
    tall = depth + 2 * HALO
    chunks = cols // CHUNK
    ky = lax.axis_index("gy")
    kz = lax.axis_index("gz")

    def at(y, z):
        return {"gy": y, "gz": z}

    def exists(dy, dz):
        ok = True
        if dy:
            ok = (ky + dy >= 0) & (ky + dy < ny)
        if dz:
            ok = ok & (kz + dz >= 0) & (kz + dz < nz)
        return ok

    def partner(r):
        size = 2 ** r
        bit = lax.rem(lax.div(ky, size), 2)
        return bit, ky + size * (1 - 2 * bit)

    barrier = pltpu.get_barrier_semaphore()
    expected = jnp.int32(rounds)
    for dy, dz in DIRECTIONS:
        ok = exists(dy, dz)
        expected = expected + jnp.where(ok, 1, 0)

        @pl.when(ok)
        def _(dy=dy, dz=dz):
            pl.semaphore_signal(barrier, inc=1, device_id=at(ky + dy, kz + dz), device_id_type=MESH)

    for r in range(rounds):
        pl.semaphore_signal(barrier, inc=1, device_id=at(partner(r)[1], kz), device_id_type=MESH)
    pl.semaphore_wait(barrier, expected)

    left = kz < nz // 2
    inward = jnp.where(left, 1, -1)
    order = jnp.where(left, kz, nz - 1 - kz)
    middle = order == nz // 2 - 1
    outermost = order == 0
    slot_out = jnp.where(middle, 1, 0)

    lane = lax.broadcasted_iota(jnp.int32, (STENCIL_ROWS, nx), 1)
    keep = {s: (lane >= s) if s > 0 else (lane < nx + s) for s in (-2, -1, 1, 2)}

    def shifted(value, s):
        return jnp.where(keep[s], pltpu.roll(value, s % nx, 1), 0.0)

    contrast = con[...]
    squared = jnp.broadcast_to(contrast * contrast, (STENCIL_ROWS, nx))
    t_ref[0:8, :] = jnp.zeros((8, nx), jnp.float32)
    t_ref[rows + 8:rows + 16, :] = jnp.zeros((8, nx), jnp.float32)
    out[...] = vol[...]

    out2 = out.reshape(depth * nx, cols)
    dt2 = dt_ref.reshape(depth * nx, cols)
    vx2 = vx_ref.reshape(depth * nx, cols)
    vy2 = vy_ref.reshape(depth * cols, nx)
    d2 = d_ref.reshape((depth + 2) * rows, nx)

    def step_body(step, carry):
        c4 = c_ref.at[step]
        c2 = c4.reshape(tall * rows, nx)

        @pl.loop(0, depth)
        def _(z):
            c4[z + HALO, PAD:PAD + cols, :] = out[z].T

        def halo(i):
            dy, dz = DIRECTIONS[i]
            src_y = {0: (PAD, cols), 1: (cols, PAD), -1: (PAD, PAD)}[dy]
            dst_y = {0: (PAD, cols), 1: (0, PAD), -1: (PAD + cols, PAD)}[dy]
            src_z = {0: (HALO, depth), 1: (depth, HALO), -1: (HALO, HALO)}[dz]
            dst_z = {0: (HALO, depth), 1: (0, HALO), -1: (HALO + depth, HALO)}[dz]
            src = c4.at[pl.ds(*src_z), pl.ds(*src_y), :]
            dst = c4.at[pl.ds(*dst_z), pl.ds(*dst_y), :]
            copy = pltpu.make_async_remote_copy(
                src_ref=src, dst_ref=dst, send_sem=halo_s.at[step, i], recv_sem=halo_r.at[step, i],
                device_id=at(ky + dy, kz + dz), device_id_type=MESH)
            return copy, dst_z, dst_y

        for i, (dy, dz) in enumerate(DIRECTIONS):
            copy, dst_z, dst_y = halo(i)

            @pl.when(exists(dy, dz))
            def _(copy=copy):
                copy.start()

            @pl.when(jnp.logical_not(exists(-dy, -dz)))
            def _(dst_z=dst_z, dst_y=dst_y):
                c4[pl.ds(*dst_z), pl.ds(*dst_y), :] = jnp.zeros((dst_z[1], dst_y[1], nx), jnp.float32)

        for i, (dy, dz) in enumerate(DIRECTIONS):
            copy = halo(i)[0]

            @pl.when(exists(-dy, -dz))
            def _(copy=copy):
                copy.wait_recv()

        for i, (dy, dz) in enumerate(DIRECTIONS):
            copy = halo(i)[0]

            @pl.when(exists(dy, dz))
            def _(copy=copy):
                copy.wait_send()

        @pl.loop(0, depth + 4)
        def _(z):
            for r0 in range(0, rows, STENCIL_ROWS):
                part = pl.ds(r0, STENCIL_ROWS)
                total = TAPS[2] * c4[z + 2, part, :]
                total = total + TAPS[1] * (c4[z + 1, part, :] + c4[z + 3, part, :])
                total = total + TAPS[0] * (c4[z, part, :] + c4[z + 4, part, :])
                t_ref[pl.ds(r0 + 8, STENCIL_ROWS), :] = total
            place_z = kz * depth + z - 2
            inside_z = (place_z >= 0) & (place_z < nz * depth)
            for r0 in range(0, rows, STENCIL_ROWS):
                def tap(o):
                    return t_ref[pl.ds(r0 + 8 + o, STENCIL_ROWS), :]
                total = TAPS[2] * tap(0) + TAPS[1] * (tap(-1) + tap(1)) + TAPS[0] * (tap(-2) + tap(2))
                blurred = (TAPS[2] * total + TAPS[1] * (shifted(total, 1) + shifted(total, -1))
                           + TAPS[0] * (shifted(total, 2) + shifted(total, -2)))
                place = lax.broadcasted_iota(jnp.int32, (STENCIL_ROWS, nx), 0) + (r0 - PAD + ky * cols)
                inside = (place >= 0) & (place < ny * cols) & inside_z
                b_ref[z, pl.ds(r0 + 8, STENCIL_ROWS), :] = jnp.where(inside, blurred, 0.0)

        @pl.loop(0, depth + 2)
        def _(z):
            for r0 in range(0, rows, STENCIL_ROWS):
                part = pl.ds(r0 + 8, STENCIL_ROWS)
                mid = b_ref[z + 1, part, :]
                grad_z = b_ref[z + 2, part, :] - b_ref[z, part, :]
                grad_y = (b_ref[z + 1, pl.ds(r0 + 9, STENCIL_ROWS), :]
                          - b_ref[z + 1, pl.ds(r0 + 7, STENCIL_ROWS), :])
                grad_x = shifted(mid, -1) - shifted(mid, 1)
                square = (grad_x * grad_x + grad_y * grad_y + grad_z * grad_z) * 0.25
                d_ref[z, pl.ds(r0, STENCIL_ROWS), :] = (SCALE * squared) / (squared + square)

        @pl.loop(0, depth)
        def _(z):
            dt_ref[z] = d_ref[z + 1, PAD:PAD + cols, :].T

        @pl.loop(0, chunks)
        def _(c):
            y0 = pl.multiple_of(c * CHUNK, CHUNK)
            part = pl.ds(y0 + PAD, CHUNK)
            own = pl.ds(y0, CHUNK)
            d = d_ref[1, part, :]
            f_lo = jnp.where(kz > 0, d_ref[0, part, :] + d, 0.0)
            d_next = d_ref[2, part, :]
            g = d + d_next
            d = d_next
            ea = jnp.ones_like(g)
            ra = c4[HALO, part, :]
            e = ea
            r = c4[HALO + 1, part, :]
            for i in range(1, depth - 1):
                d_next = d_ref[i + 2, part, :]
                f = d + d_next
                d = d_next
                s = 1.0 / (e + g + f)
                wf, wg = f * s, g * s
                wz_ref[0, i, own, :] = wf
                wz_ref[1, i, own, :] = wg
                wz_ref[2, i, own, :] = r * s
                ea = ea + wg * e
                ra = ra + wg * r
                e = 1.0 + wf * e
                r = c4[HALO + i + 1, part, :] + wf * r
                g = wf * g
            f_hi = jnp.where(kz < nz - 1, d + d_ref[depth + 1, part, :], 0.0)
            zr_ref[0, own, :] = jnp.where(left, ea, e)
            zr_ref[1, own, :] = jnp.where(left, ra, r)
            zr_ref[2, own, :] = jnp.where(left, e, ea)
            zr_ref[3, own, :] = jnp.where(left, r, ra)
            zr_ref[4, own, :] = g
            zr_ref[5, own, :] = jnp.where(left, f_hi, f_lo)

        def z_copy(c, slot):
            return pltpu.make_async_remote_copy(
                src_ref=zsend.at[step, c], dst_ref=zbuf.at[step, slot, c], send_sem=zs.at[step, c],
                recv_sem=zrs.at[step, slot, c], device_id=at(ky, kz + inward), device_id_type=MESH)

        def z_back(c):
            return pltpu.make_async_remote_copy(
                src_ref=zvsend.at[step, c], dst_ref=zv.at[step, c], send_sem=zvs.at[step, c],
                recv_sem=zvr.at[step, c], device_id=at(ky, kz - inward), device_id_type=MESH)

        def z_inward(c, carry):
            own = pl.ds(pl.multiple_of(c * CHUNK, CHUNK), CHUNK)

            @pl.when(jnp.logical_not(outermost))
            def _():
                z_copy(c, 0).wait_recv()
                zr_ref[0, own, :] += zbuf[step, 0, c, 0]
                zr_ref[1, own, :] += zbuf[step, 0, c, 1]

            eo, ro, ei, ri, g, f = [zr_ref[j, own, :] for j in range(6)]
            s = 1.0 / (eo + g)
            w = g * s
            ei = ei + w * eo
            ri = ri + w * ro
            s2 = 1.0 / (ei + f)
            u = f * s2
            zi_ref[0, own, :] = w
            zi_ref[1, own, :] = ro * s
            zi_ref[2, own, :] = ei
            zi_ref[3, own, :] = ri
            zi_ref[4, own, :] = u
            zi_ref[5, own, :] = ri * s2
            zsend[step, c, 0] = u * ei
            zsend[step, c, 1] = u * ri
            z_copy(c, slot_out).start()
            return carry

        def z_outward(c, carry):
            own = pl.ds(pl.multiple_of(c * CHUNK, CHUNK), CHUNK)

            @pl.when(middle)
            def _():
                z_copy(c, 1).wait_recv()
                zr_ref[0, own, :] = (zi_ref[3, own, :] + zbuf[step, 1, c, 1]) / (zi_ref[2, own, :] + zbuf[step, 1, c, 0])

            @pl.when(jnp.logical_not(middle))
            def _():
                z_back(c).wait_recv()
                zr_ref[0, own, :] = zi_ref[4, own, :] * zv[step, c] + zi_ref[5, own, :]

            vi = zr_ref[0, own, :]
            vo = zi_ref[0, own, :] * vi + zi_ref[1, own, :]

            @pl.when(jnp.logical_not(outermost))
            def _():
                zvsend[step, c] = vo
                z_back(c).start()

            va = jnp.where(left, vo, vi)
            v = jnp.where(left, vi, vo)
            vz_ref[0, own, :] = va
            vz_ref[depth - 1, own, :] = v
            for i in range(depth - 2, 0, -1):
                v = wz_ref[0, i, own, :] * v + (wz_ref[1, i, own, :] * va + wz_ref[2, i, own, :])
                vz_ref[i, own, :] = v
            return carry

        @pl.when(outermost)
        def _():
            lax.fori_loop(0, chunks, z_inward, 0)

        def dx(i):
            return dt2[pl.ds(i, depth, stride=nx), :]

        def rx(i):
            return out2[pl.ds(i, depth, stride=nx), :]

        def dy_(i):
            return d2[pl.ds(i + rows + PAD, depth, stride=rows), :]

        def ry(i):
            return c2[pl.ds(i + HALO * rows + PAD, depth, stride=rows), :]

        half_x = nx // 2
        half_y = cols // 2

        def x_reduce(i, state):
            el, rl, dl, er, rr, dr = state
            j = nx - 1 - i
            d1 = dx(i + 1)
            d3 = dx(j - 1)
            fl = dl + d1
            fr = dr + d3
            sl = 1.0 / (el + fl)
            sr = 1.0 / (er + fr)
            wl = fl * sl
            wr = fr * sr
            wx_ref[0, i] = wl
            wx_ref[1, i] = rl * sl
            wx_ref[0, j] = wr
            wx_ref[1, j] = rr * sr
            return (1.0 + wl * el, rx(i + 1) + wl * rl, d1, 1.0 + wr * er, rx(j - 1) + wr * rr, d3)

        def y_first(base):
            d0, d1 = dy_(base), dy_(base + 1)
            one = jnp.ones_like(d0)
            return (one, ry(base), d0 + d1, one, ry(base + 1), d1)

        def y_reduce(i, state, base):
            ea, ra, g, e, r, d = state
            d1 = dy_(base + i + 1)
            f = d + d1
            s = 1.0 / (e + g + f)
            wf, wg = f * s, g * s
            wy_ref[0, base + i] = wf
            wy_ref[1, base + i] = wg
            wy_ref[2, base + i] = r * s
            return (ea + wg * e, ra + wg * r, wf * g, 1.0 + wf * e, ry(base + i + 1) + wf * r, d1)

        def y_body(i, states):
            return tuple(y_reduce(i, s, b) for s, b in zip(states, (0, half_y)))

        low, high = lax.fori_loop(1, half_y - 1, y_body, (y_first(0), y_first(half_y)))

        def y_chain(state, f):
            ea, ra, g, e, r, d = state
            return (ea, ra, e, r, g, f)

        chain_low = y_chain(low, low[5] + dy_(half_y))
        chain_high = y_chain(high, jnp.where(ky < ny - 1, high[5] + dy_(cols), 0.0))
        chain, local_weights = merge(chain_low, chain_high)

        def y_copy(r):
            return pltpu.make_async_remote_copy(
                src_ref=ysend.at[step, r], dst_ref=yrecv.at[step, r], send_sem=ys.at[step, r],
                recv_sem=yr.at[step, r], device_id=at(partner(r)[1], kz), device_id_type=MESH)

        def y_start(r, chain):
            for j in range(6):
                ysend[step, r, j] = chain[j]
            y_copy(r).start()

        if rounds:
            y_start(0, chain)

        @pl.when(jnp.logical_not(outermost))
        def _():
            lax.fori_loop(0, chunks, z_inward, 0)

        zero = jnp.zeros((depth, cols), jnp.float32)
        state = lax.fori_loop(0, half_x - 1, x_reduce, (zero + 1.0, rx(0), dx(0), zero + 1.0, rx(nx - 1), dx(nx - 1)))
        el, rl, dl, er, rr, dr = state
        x_ends = solve_pair(el, rl, er, rr, dl + dr)

        weights = []
        for r in range(rounds):
            y_copy(r).wait_recv()
            other = tuple(yrecv[step, r, j] for j in range(6))
            first = partner(r)[0] == 0
            pair_l = tuple(jnp.where(first, a, b) for a, b in zip(chain, other))
            pair_r = tuple(jnp.where(first, b, a) for a, b in zip(chain, other))
            chain, w = merge(pair_l, pair_r)
            weights.append(w)
            if r + 1 < rounds:
                y_start(r + 1, chain)

        va, vb = solve_pair(*chain[:5])
        for r in range(rounds - 1, -1, -1):
            first = partner(r)[0] == 0
            inner_l, inner_r = unmerge(weights[r], va, vb)
            va = jnp.where(first, va, inner_r)
            vb = jnp.where(first, inner_l, vb)
        inner_l, inner_r = unmerge(local_weights, va, vb)

        def put_x(i, v):
            vx2[pl.ds(i, depth, stride=nx), :] = v

        def put_y(i, v):
            vy2[pl.ds(i, depth, stride=cols), :] = v

        put_x(half_x - 1, x_ends[0])
        put_x(half_x, x_ends[1])
        put_y(0, va)
        put_y(half_y - 1, inner_l)
        put_y(half_y, inner_r)
        put_y(cols - 1, vb)

        def x_back(k, state):
            vl, vr = state
            i = half_x - 2 - k
            j = half_x + 1 + k
            vl = wx_ref[0, i] * vl + wx_ref[1, i]
            vr = wx_ref[0, j] * vr + wx_ref[1, j]
            put_x(i, vl)
            put_x(j, vr)
            return vl, vr

        lax.fori_loop(0, half_x - 1, x_back, x_ends)

        def y_back(k, state):
            vl, vr = state
            i = half_y - 2 - k
            vl = wy_ref[0, i] * vl + (wy_ref[1, i] * va + wy_ref[2, i])
            j = i + half_y
            vr = wy_ref[0, j] * vr + (wy_ref[1, j] * inner_r + wy_ref[2, j])
            put_y(i, vl)
            put_y(j, vr)
            return vl, vr

        lax.fori_loop(0, half_y - 2, y_back, (inner_l, vb))

        lax.fori_loop(0, chunks, z_outward, 0)

        @pl.loop(0, depth)
        def _(z):
            out[z] = (vx_ref[z] + (vy_ref[z] + vz_ref[z]).T) * (1.0 / 3.0)

        for r in range(rounds):
            y_copy(r).wait_send()

        @pl.loop(0, chunks)
        def _(c):
            z_copy(c, slot_out).wait_send()

            @pl.when(jnp.logical_not(outermost))
            def _():
                z_back(c).wait_send()

        return carry

    lax.fori_loop(0, STEPS, step_body, 0)


def on_device(volume, contrast):
    depth, nx, cols = volume.shape
    ny = lax.axis_size("gy")
    nz = lax.axis_size("gz")
    rounds = ny.bit_length() - 1
    assert 2 ** rounds == ny and nz % 2 == 0 and nz >= 2
    rows = cols + 2 * PAD
    chunks = cols // CHUNK
    f32 = jnp.float32
    dma = pltpu.SemaphoreType.DMA
    count = len(DIRECTIONS)
    return pl.pallas_call(
        functools.partial(kernel, ny, nz, rounds),
        out_shape=jax.ShapeDtypeStruct(volume.shape, f32),
        in_specs=[pl.BlockSpec(memory_space=pltpu.VMEM)] * 2,
        out_specs=pl.BlockSpec(memory_space=pltpu.VMEM),
        scratch_shapes=[
            pltpu.VMEM((STEPS, depth + 2 * HALO, rows, nx), f32),
            pltpu.VMEM((rows + 16, nx), f32),
            pltpu.VMEM((depth + 4, rows + 16, nx), f32),
            pltpu.VMEM((depth + 2, rows, nx), f32),
            pltpu.VMEM((depth, nx, cols), f32),
            pltpu.VMEM((2, nx, depth, cols), f32),
            pltpu.VMEM((3, cols, depth, nx), f32),
            pltpu.VMEM((3, depth, cols, nx), f32),
            pltpu.VMEM((depth, nx, cols), f32),
            pltpu.VMEM((depth, cols, nx), f32),
            pltpu.VMEM((depth, cols, nx), f32),
            pltpu.VMEM((6, cols, nx), f32),
            pltpu.VMEM((6, cols, nx), f32),
            pltpu.VMEM((STEPS, chunks, 2, CHUNK, nx), f32),
            pltpu.VMEM((STEPS, 2, chunks, 2, CHUNK, nx), f32),
            pltpu.VMEM((STEPS, chunks, CHUNK, nx), f32),
            pltpu.VMEM((STEPS, chunks, CHUNK, nx), f32),
            pltpu.VMEM((STEPS, max(rounds, 1), 6, depth, nx), f32),
            pltpu.VMEM((STEPS, max(rounds, 1), 6, depth, nx), f32),
            dma((STEPS, count)), dma((STEPS, count)),
            dma((STEPS, chunks)), dma((STEPS, 2, chunks)),
            dma((STEPS, chunks)), dma((STEPS, chunks)),
            dma((STEPS, max(rounds, 1))), dma((STEPS, max(rounds, 1))),
        ],
        compiler_params=pltpu.CompilerParams(
            collective_id=0, has_side_effects=True, vmem_limit_bytes=48 * 2 ** 20
        ),
    )(volume, contrast.reshape(1, nx))


def solution(mesh):
    in_specs = (P("gz", None, "gy"), P())
    out_specs = P("gz", None, "gy")
    return jax.shard_map(
        on_device, mesh=mesh, in_specs=in_specs, out_specs=out_specs, check_vma=False
    )
```

```python
import functools

import jax
import jax.numpy as jnp
from jax import lax
from jax.experimental import pallas as pl
from jax.experimental.pallas import tpu as pltpu
from jax.sharding import PartitionSpec as P

STEPS = 2
TAPS = (0.05448868, 0.24420134, 0.40261995, 0.24420134, 0.05448868)
SCALE = 600.0
MESH = pl.DeviceIdType.MESH
DIRECTIONS = [(dy, dz) for dz in (-1, 1, 0) for dy in (0, -1, 1) if (dy, dz) != (0, 0)]
PAD = 8
HALO = 4
CHUNK = 32
STENCIL_ROWS = 48
SEGMENTS = 4


def merge(left, right):
    ea, ra, eb, rb, g, f = left
    ea2, ra2, eb2, rb2, g2, f2 = right
    s1 = 1.0 / (eb + g + f)
    wg, wf, q1 = g * s1, f * s1, rb * s1
    ea = ea + wg * eb
    ra = ra + wg * rb
    ea2 = ea2 + wf * eb
    ra2 = ra2 + wf * rb
    g1 = wf * g
    s2 = 1.0 / (ea2 + g1 + g2)
    vg, vf, q2 = g1 * s2, g2 * s2, ra2 * s2
    joined = (ea + vg * ea2, ra + vg * ra2, eb2 + vf * ea2, rb2 + vf * ra2, vf * g1, f2)
    return joined, (wg, wf, q1, vg, vf, q2)


def unmerge(weights, va, vb):
    wg, wf, q1, vg, vf, q2 = weights
    inner_right = vg * va + vf * vb + q2
    inner_left = wg * va + wf * inner_right + q1
    return inner_left, inner_right


def solve_pair(ea, ra, eb, rb, g):
    s = 1.0 / (ea + g)
    w = g * s
    vb = (rb + w * ra) / (eb + w * ea)
    return w * vb + ra * s, vb


def merge_all(chains):
    levels = []
    while len(chains) > 1:
        pairs = [merge(chains[i], chains[i + 1]) for i in range(0, len(chains), 2)]
        chains = [p[0] for p in pairs]
        levels.append([p[1] for p in pairs])
    return chains[0], levels


def unmerge_all(levels, va, vb):
    ends = [(va, vb)]
    for level in reversed(levels):
        split = []
        for weights, (a, b) in zip(level, ends):
            inner_left, inner_right = unmerge(weights, a, b)
            split += [(a, inner_left), (inner_right, b)]
        ends = split
    return ends


def line_start(get_d, get_r, count):
    states = []
    for base in range(0, count, count // SEGMENTS):
        d0, d1 = get_d(base), get_d(base + 1)
        one = jnp.ones_like(d0)
        states.append((one, get_r(base), d0 + d1, one, get_r(base + 1), d1))
    return tuple(states)


def line_reduce(get_d, get_r, weights, count, first, last, states):
    size = count // SEGMENTS

    def body(i, states):
        new = []
        for k, (ea, ra, g, e, r, d) in enumerate(states):
            j = k * size + i
            d1 = get_d(j + 1)
            f = d + d1
            s = 1.0 / (e + g + f)
            wf, wg = f * s, g * s
            weights[0, j] = wf
            weights[1, j] = wg
            weights[2, j] = r * s
            new.append((ea + wg * e, ra + wg * r, wf * g, 1.0 + wf * e, get_r(j + 1) + wf * r, d1))
        return tuple(new)

    return lax.fori_loop(first, last, body, states)


def line_chain(get_d, states, count, edge):
    size = count // SEGMENTS
    chains = []
    for k, (ea, ra, g, e, r, d) in enumerate(states):
        f = d + get_d((k + 1) * size) if k + 1 < SEGMENTS else edge(d)
        chains.append((ea, ra, e, r, g, f))
    return merge_all(chains)


def line_back(put, weights, count, ends):
    size = count // SEGMENTS
    for k, (a, b) in enumerate(ends):
        put(k * size, a)
        put(k * size + size - 1, b)

    def body(t, values):
        new = []
        for k, v in enumerate(values):
            j = k * size + size - 2 - t
            v = weights[0, j] * v + (weights[1, j] * ends[k][0] + weights[2, j])
            put(j, v)
            new.append(v)
        return tuple(new)

    lax.fori_loop(0, size - 2, body, tuple(b for a, b in ends))


def kernel(ny, nz, rounds, vol, con, out, c_ref, t_ref, b_ref, d_ref, dt_ref, wx_ref, wy_ref, wz_ref, vx_ref, vy_ref,
           vz_ref, zr_ref, zi_ref, zsend, zbuf, zvsend, zv, ysend, yrecv,
           halo_s, halo_r, zs, zrs, zvs, zvr, ys, yr):
    depth, nx, cols = vol.shape
    rows = cols + 2 * PAD
    tall = depth + 2 * HALO
    chunks = cols // CHUNK
    ky = lax.axis_index("gy")
    kz = lax.axis_index("gz")

    def at(y, z):
        return {"gy": y, "gz": z}

    def exists(dy, dz):
        ok = True
        if dy:
            ok = (ky + dy >= 0) & (ky + dy < ny)
        if dz:
            ok = ok & (kz + dz >= 0) & (kz + dz < nz)
        return ok

    def partner(r):
        size = 2 ** r
        bit = lax.rem(lax.div(ky, size), 2)
        return bit, ky + size * (1 - 2 * bit)

    barrier = pltpu.get_barrier_semaphore()
    expected = jnp.int32(rounds)
    for dy, dz in DIRECTIONS:
        ok = exists(dy, dz)
        expected = expected + jnp.where(ok, 1, 0)

        @pl.when(ok)
        def _(dy=dy, dz=dz):
            pl.semaphore_signal(barrier, inc=1, device_id=at(ky + dy, kz + dz), device_id_type=MESH)

    for r in range(rounds):
        pl.semaphore_signal(barrier, inc=1, device_id=at(partner(r)[1], kz), device_id_type=MESH)
    @pl.loop(0, depth // 4)
    def _(k):
        for z in [4 * k, 4 * k + 1, 4 * k + 2, 4 * k + 3]:
            plane = vol[z]
            out[z] = plane
            c_ref[0, z + HALO, PAD:PAD + cols, :] = plane.T

    pl.semaphore_wait(barrier, expected)

    left = kz < nz // 2
    inward = jnp.where(left, 1, -1)
    order = jnp.where(left, kz, nz - 1 - kz)
    middle = order == nz // 2 - 1
    outermost = order == 0
    slot_out = jnp.where(middle, 1, 0)

    lane = lax.broadcasted_iota(jnp.int32, (STENCIL_ROWS, nx), 1)
    keep = {s: (lane >= s) if s > 0 else (lane < nx + s) for s in (-2, -1, 1, 2)}

    def shifted(value, s):
        return jnp.where(keep[s][:value.shape[0]], pltpu.roll(value, s % nx, 1), 0.0)

    contrast = con[...]
    squared = jnp.broadcast_to(contrast * contrast, (STENCIL_ROWS, nx))
    t_ref[0:8, :] = jnp.zeros((8, nx), jnp.float32)
    t_ref[rows + 8:rows + 16, :] = jnp.zeros((8, nx), jnp.float32)

    out2 = out.reshape(depth * nx, cols)
    dt2 = dt_ref.reshape(depth * nx, cols)
    vx2 = vx_ref.reshape(depth * nx, cols)
    vy2 = vy_ref.reshape(depth * cols, nx)
    d2 = d_ref.reshape((depth + 2) * rows, nx)

    def finish(z, target):
        plane = (vx_ref[z] + (vy_ref[z] + vz_ref[z]).T) * (1.0 / 3.0)
        out[z] = plane
        if target is not None:
            target[z + HALO, PAD:PAD + cols, :] = plane.T

    def finish_edges(target):
        @pl.loop(0, HALO // 2)
        def _(k):
            for t in range(2):
                finish(2 * k + t, target)
                finish(depth - HALO + 2 * k + t, target)

    def finish_middle(target):
        @pl.loop(0, (depth - 2 * HALO) // 4)
        def _(k):
            for t in range(4):
                finish(HALO + 4 * k + t, target)

    parts = [(r0, min(STENCIL_ROWS, cols + 8 - r0)) for r0 in range(0, cols + 8, STENCIL_ROWS)]

    for step in range(STEPS):
        c4 = c_ref.at[step]
        c2 = c4.reshape(tall * rows, nx)

        def halo(i, c4=c4, step=step):
            dy, dz = DIRECTIONS[i]
            src_y = {0: (PAD, cols), 1: (cols, PAD), -1: (PAD, PAD)}[dy]
            dst_y = {0: (PAD, cols), 1: (0, PAD), -1: (PAD + cols, PAD)}[dy]
            src_z = {0: (HALO, depth), 1: (depth, HALO), -1: (HALO, HALO)}[dz]
            dst_z = {0: (HALO, depth), 1: (0, HALO), -1: (HALO + depth, HALO)}[dz]
            src = c4.at[pl.ds(*src_z), pl.ds(*src_y), :]
            dst = c4.at[pl.ds(*dst_z), pl.ds(*dst_y), :]
            copy = pltpu.make_async_remote_copy(
                src_ref=src, dst_ref=dst, send_sem=halo_s.at[step, i], recv_sem=halo_r.at[step, i],
                device_id=at(ky + dy, kz + dz), device_id_type=MESH)
            return copy, dst_z, dst_y

        def send(layers, halo=halo, c4=c4):
            for i, (dy, dz) in enumerate(DIRECTIONS):
                if (dz != 0) != layers:
                    continue
                copy, dst_z, dst_y = halo(i)

                @pl.when(exists(dy, dz))
                def _(copy=copy):
                    copy.start()

                @pl.when(jnp.logical_not(exists(-dy, -dz)))
                def _(dst_z=dst_z, dst_y=dst_y):
                    c4[pl.ds(*dst_z), pl.ds(*dst_y), :] = jnp.zeros((dst_z[1], dst_y[1], nx), jnp.float32)

        def receive(layers):
            for i, (dy, dz) in enumerate(DIRECTIONS):
                if (dz != 0) != layers:
                    continue
                copy = halo(i)[0]

                @pl.when(exists(-dy, -dz))
                def _(copy=copy):
                    copy.wait_recv()

        if step == 0:
            send(True)
        else:
            finish_edges(c4)
            send(True)
            finish_middle(c4)
        send(False)

        def blur(z0, z1):
            @pl.loop(z0, z1)
            def _(z):
                for r0 in range(0, rows, STENCIL_ROWS):
                    part = pl.ds(r0, STENCIL_ROWS)
                    total = TAPS[2] * c4[z + 2, part, :]
                    total = total + TAPS[1] * (c4[z + 1, part, :] + c4[z + 3, part, :])
                    total = total + TAPS[0] * (c4[z, part, :] + c4[z + 4, part, :])
                    t_ref[pl.ds(r0 + 8, STENCIL_ROWS), :] = total
                for r0, size in parts:
                    def tap(o):
                        return t_ref[pl.ds(r0 + 12 + o, size), :]
                    total = TAPS[2] * tap(0) + TAPS[1] * (tap(-1) + tap(1)) + TAPS[0] * (tap(-2) + tap(2))
                    b_ref[z, pl.ds(r0, size), :] = (
                        TAPS[2] * total + TAPS[1] * (shifted(total, 1) + shifted(total, -1))
                        + TAPS[0] * (shifted(total, 2) + shifted(total, -2)))

            @pl.when(ky == 0)
            def _():
                b_ref[z0:z1, PAD - 5:PAD - 4, :] = jnp.zeros((z1 - z0, 1, nx), jnp.float32)

            @pl.when(ky == ny - 1)
            def _():
                b_ref[z0:z1, cols + PAD - 4:cols + PAD - 3, :] = jnp.zeros((z1 - z0, 1, nx), jnp.float32)

        def diffuse(z0, z1):
            @pl.loop(z0, z1)
            def _(z):
                for r0, size in parts:
                    mid = b_ref[z + 1, pl.ds(r0 + 4, size), :]
                    grad_z = b_ref[z + 2, pl.ds(r0 + 4, size), :] - b_ref[z, pl.ds(r0 + 4, size), :]
                    grad_y = b_ref[z + 1, pl.ds(r0 + 5, size), :] - b_ref[z + 1, pl.ds(r0 + 3, size), :]
                    grad_x = shifted(mid, -1) - shifted(mid, 1)
                    square = (grad_x * grad_x + grad_y * grad_y + grad_z * grad_z) * 0.25
                    d_ref[z, pl.ds(r0 + PAD, size), :] = (SCALE * squared[:size]) / (squared[:size] + square)

        def turn(z0, z1):
            step_by = 2 if (z1 - z0) % 2 == 0 else 1

            @pl.loop(0, (z1 - z0) // step_by)
            def _(k):
                for t in range(step_by):
                    z = z0 + k * step_by + t
                    dt_ref[z] = d_ref[z + 1, PAD:PAD + cols, :].T

        receive(False)
        blur(HALO, depth)
        diffuse(HALO, depth - 2)
        turn(HALO - 1, depth - 3)
        receive(True)
        blur(0, HALO)
        blur(depth, depth + 4)

        @pl.when(kz == 0)
        def _():
            b_ref[1] = jnp.zeros(b_ref.shape[1:], jnp.float32)

        @pl.when(kz == nz - 1)
        def _():
            b_ref[depth + 2] = jnp.zeros(b_ref.shape[1:], jnp.float32)

        diffuse(0, HALO)
        diffuse(depth - 2, depth + 2)
        turn(0, HALO - 1)
        turn(depth - 3, depth)

        for i, (dy, dz) in enumerate(DIRECTIONS):
            copy = halo(i)[0]

            @pl.when(exists(dy, dz))
            def _(copy=copy):
                copy.wait_send()

        def z_copy(c, slot):
            return pltpu.make_async_remote_copy(
                src_ref=zsend.at[step, c], dst_ref=zbuf.at[step, slot, c], send_sem=zs.at[step, c],
                recv_sem=zrs.at[step, slot, c], device_id=at(ky, kz + inward), device_id_type=MESH)

        def z_back(c):
            return pltpu.make_async_remote_copy(
                src_ref=zvsend.at[step, c], dst_ref=zv.at[step, c], send_sem=zvs.at[step, c],
                recv_sem=zvr.at[step, c], device_id=at(ky, kz - inward), device_id_type=MESH)

        def z_inward(c, carry):
            own = pl.ds(pl.multiple_of(c * CHUNK, CHUNK), CHUNK)

            @pl.when(jnp.logical_not(outermost))
            def _():
                z_copy(c, 0).wait_recv()
                zr_ref[0, own, :] += zbuf[step, 0, c, 0]
                zr_ref[1, own, :] += zbuf[step, 0, c, 1]

            eo, ro, ei, ri, g, f = [zr_ref[j, own, :] for j in range(6)]
            s = 1.0 / (eo + g)
            w = g * s
            ei = ei + w * eo
            ri = ri + w * ro
            s2 = 1.0 / (ei + f)
            u = f * s2
            zi_ref[0, own, :] = w
            zi_ref[1, own, :] = ro * s
            zi_ref[2, own, :] = ei
            zi_ref[3, own, :] = ri
            zi_ref[4, own, :] = u
            zi_ref[5, own, :] = ri * s2
            zsend[step, c, 0] = u * ei
            zsend[step, c, 1] = u * ri
            z_copy(c, slot_out).start()
            return carry

        def z_outward(c, carry):
            own = pl.ds(pl.multiple_of(c * CHUNK, CHUNK), CHUNK)

            @pl.when(middle)
            def _():
                z_copy(c, 1).wait_recv()
                zr_ref[0, own, :] = (zi_ref[3, own, :] + zbuf[step, 1, c, 1]) / (zi_ref[2, own, :] + zbuf[step, 1, c, 0])

            @pl.when(jnp.logical_not(middle))
            def _():
                z_back(c).wait_recv()
                zr_ref[0, own, :] = zi_ref[4, own, :] * zv[step, c] + zi_ref[5, own, :]

            vi = zr_ref[0, own, :]
            vo = zi_ref[0, own, :] * vi + zi_ref[1, own, :]

            @pl.when(jnp.logical_not(outermost))
            def _():
                zvsend[step, c] = vo
                z_back(c).start()

            va = jnp.where(left, vo, vi)
            v = jnp.where(left, vi, vo)
            vz_ref[0, own, :] = va
            vz_ref[depth - 1, own, :] = v
            for i in range(depth - 2, 0, -1):
                v = wz_ref[0, i, own, :] * v + (wz_ref[1, i, own, :] * va + wz_ref[2, i, own, :])
                vz_ref[i, own, :] = v
            return carry

        @pl.loop(0, chunks)
        def _(c):
            y0 = pl.multiple_of(c * CHUNK, CHUNK)
            part = pl.ds(y0 + PAD, CHUNK)
            own = pl.ds(y0, CHUNK)
            d = d_ref[1, part, :]
            f_lo = jnp.where(kz > 0, d_ref[0, part, :] + d, 0.0)
            d_next = d_ref[2, part, :]
            g = d + d_next
            d = d_next
            ea = jnp.ones_like(g)
            ra = c4[HALO, part, :]
            e = ea
            r = c4[HALO + 1, part, :]
            for i in range(1, depth - 1):
                d_next = d_ref[i + 2, part, :]
                f = d + d_next
                d = d_next
                s = 1.0 / (e + g + f)
                wf, wg = f * s, g * s
                wz_ref[0, i, own, :] = wf
                wz_ref[1, i, own, :] = wg
                wz_ref[2, i, own, :] = r * s
                ea = ea + wg * e
                ra = ra + wg * r
                e = 1.0 + wf * e
                r = c4[HALO + i + 1, part, :] + wf * r
                g = wf * g
            f_hi = jnp.where(kz < nz - 1, d + d_ref[depth + 1, part, :], 0.0)
            zr_ref[0, own, :] = jnp.where(left, ea, e)
            zr_ref[1, own, :] = jnp.where(left, ra, r)
            zr_ref[2, own, :] = jnp.where(left, e, ea)
            zr_ref[3, own, :] = jnp.where(left, r, ra)
            zr_ref[4, own, :] = g
            zr_ref[5, own, :] = jnp.where(left, f_hi, f_lo)

            @pl.when(outermost)
            def _():
                z_inward(c, 0)


        def dx(i):
            return dt2[pl.ds(i, depth, stride=nx), :]

        def rx(i):
            return out2[pl.ds(i, depth, stride=nx), :]

        def dy_(i):
            return d2[pl.ds(i + rows + PAD, depth, stride=rows), :]

        def ry(i):
            return c2[pl.ds(i + HALO * rows + PAD, depth, stride=rows), :]

        def put_x(i, v):
            vx2[pl.ds(i, depth, stride=nx), :] = v

        def put_y(i, v):
            vy2[pl.ds(i, depth, stride=cols), :] = v

        states = line_start(dy_, ry, cols)
        states = line_reduce(dy_, ry, wy_ref, cols, 1, cols // SEGMENTS - 1, states)
        chain, levels_y = line_chain(
            dy_, states, cols, lambda d: jnp.where(ky < ny - 1, d + dy_(cols), 0.0))

        def y_copy(r):
            return pltpu.make_async_remote_copy(
                src_ref=ysend.at[step, r], dst_ref=yrecv.at[step, r], send_sem=ys.at[step, r],
                recv_sem=yr.at[step, r], device_id=at(partner(r)[1], kz), device_id_type=MESH)

        def y_start(r, chain):
            for j in range(6):
                ysend[step, r, j] = chain[j]
            y_copy(r).start()

        if rounds:
            y_start(0, chain)

        half = nx // SEGMENTS // 2
        states = line_start(dx, rx, nx)
        states = line_reduce(dx, rx, wx_ref, nx, 1, half, states)

        @pl.when(jnp.logical_not(outermost))
        def _():
            lax.fori_loop(0, chunks, z_inward, 0)

        weights = []

        def y_round(r, chain):
            y_copy(r).wait_recv()
            other = tuple(yrecv[step, r, j] for j in range(6))
            first = partner(r)[0] == 0
            pair_l = tuple(jnp.where(first, a, b) for a, b in zip(chain, other))
            pair_r = tuple(jnp.where(first, b, a) for a, b in zip(chain, other))
            chain, w = merge(pair_l, pair_r)
            weights.append(w)
            if r + 1 < rounds:
                y_start(r + 1, chain)
            return chain

        if rounds > 0:
            chain = y_round(0, chain)
        states = line_reduce(dx, rx, wx_ref, nx, half, nx // SEGMENTS - 1, states)
        x_chain, levels_x = line_chain(dx, states, nx, jnp.zeros_like)
        if rounds > 1:
            chain = y_round(1, chain)
        line_back(put_x, wx_ref, nx, unmerge_all(levels_x, *solve_pair(*x_chain[:5])))

        @pl.when(jnp.logical_not(outermost))
        def _():
            lax.fori_loop(0, chunks, z_outward, 0)

        for r in range(2, rounds):
            chain = y_round(r, chain)

        va, vb = solve_pair(*chain[:5])
        for r in range(rounds - 1, -1, -1):
            first = partner(r)[0] == 0
            inner_l, inner_r = unmerge(weights[r], va, vb)
            va = jnp.where(first, va, inner_r)
            vb = jnp.where(first, inner_l, vb)
        line_back(put_y, wy_ref, cols, unmerge_all(levels_y, va, vb))

        @pl.when(outermost)
        def _():
            lax.fori_loop(0, chunks, z_outward, 0)

        for r in range(rounds):
            y_copy(r).wait_send()

        @pl.loop(0, chunks)
        def _(c):
            z_copy(c, slot_out).wait_send()

            @pl.when(jnp.logical_not(outermost))
            def _():
                z_back(c).wait_send()

    @pl.loop(0, depth // 4)
    def _(k):
        for t in range(4):
            finish(4 * k + t, None)


def on_device(volume, contrast):
    depth, nx, cols = volume.shape
    ny = lax.axis_size("gy")
    nz = lax.axis_size("gz")
    rounds = ny.bit_length() - 1
    assert 2 ** rounds == ny and nz % 2 == 0 and nz >= 2
    rows = cols + 2 * PAD
    chunks = cols // CHUNK
    f32 = jnp.float32
    dma = pltpu.SemaphoreType.DMA
    count = len(DIRECTIONS)
    return pl.pallas_call(
        functools.partial(kernel, ny, nz, rounds),
        out_shape=jax.ShapeDtypeStruct(volume.shape, f32),
        in_specs=[pl.BlockSpec(memory_space=pltpu.VMEM)] * 2,
        out_specs=pl.BlockSpec(memory_space=pltpu.VMEM),
        scratch_shapes=[
            pltpu.VMEM((STEPS, depth + 2 * HALO, rows, nx), f32),
            pltpu.VMEM((rows + 16, nx), f32),
            pltpu.VMEM((depth + 4, rows + 16, nx), f32),
            pltpu.VMEM((depth + 2, rows, nx), f32),
            pltpu.VMEM((depth, nx, cols), f32),
            pltpu.VMEM((3, nx, depth, cols), f32),
            pltpu.VMEM((3, cols, depth, nx), f32),
            pltpu.VMEM((3, depth, cols, nx), f32),
            pltpu.VMEM((depth, nx, cols), f32),
            pltpu.VMEM((depth, cols, nx), f32),
            pltpu.VMEM((depth, cols, nx), f32),
            pltpu.VMEM((6, cols, nx), f32),
            pltpu.VMEM((6, cols, nx), f32),
            pltpu.VMEM((STEPS, chunks, 2, CHUNK, nx), f32),
            pltpu.VMEM((STEPS, 2, chunks, 2, CHUNK, nx), f32),
            pltpu.VMEM((STEPS, chunks, CHUNK, nx), f32),
            pltpu.VMEM((STEPS, chunks, CHUNK, nx), f32),
            pltpu.VMEM((STEPS, max(rounds, 1), 6, depth, nx), f32),
            pltpu.VMEM((STEPS, max(rounds, 1), 6, depth, nx), f32),
            dma((STEPS, count)), dma((STEPS, count)),
            dma((STEPS, chunks)), dma((STEPS, 2, chunks)),
            dma((STEPS, chunks)), dma((STEPS, chunks)),
            dma((STEPS, max(rounds, 1))), dma((STEPS, max(rounds, 1))),
        ],
        compiler_params=pltpu.CompilerParams(
            collective_id=0, has_side_effects=True, vmem_limit_bytes=48 * 2 ** 20
        ),
    )(volume, contrast.reshape(1, nx))


def solution(mesh):
    in_specs = (P("gz", None, "gy"), P())
    out_specs = P("gz", None, "gy")
    return jax.shard_map(
        on_device, mesh=mesh, in_specs=in_specs, out_specs=out_specs, check_vma=False
    )
```

```python
import functools

import jax
import jax.numpy as jnp
from jax import lax
from jax.experimental import pallas as pl
from jax.experimental.pallas import tpu as pltpu
from jax.sharding import PartitionSpec as P

STEPS = 2
TAPS = (0.05448868, 0.24420134, 0.40261995, 0.24420134, 0.05448868)
SCALE = 600.0
MESH = pl.DeviceIdType.MESH
DIRECTIONS = [(dy, dz) for dz in (-1, 1, 0) for dy in (0, -1, 1) if (dy, dz) != (0, 0)]
PAD = 8
HALO = 4
CHUNK = 32
STENCIL_ROWS = 48
SEGMENTS = 4
SKEW = 8


def merge(left, right):
    ea, ra, eb, rb, g, f = left
    ea2, ra2, eb2, rb2, g2, f2 = right
    s1 = 1.0 / (eb + g + f)
    wg, wf, q1 = g * s1, f * s1, rb * s1
    ea = ea + wg * eb
    ra = ra + wg * rb
    ea2 = ea2 + wf * eb
    ra2 = ra2 + wf * rb
    g1 = wf * g
    s2 = 1.0 / (ea2 + g1 + g2)
    vg, vf, q2 = g1 * s2, g2 * s2, ra2 * s2
    joined = (ea + vg * ea2, ra + vg * ra2, eb2 + vf * ea2, rb2 + vf * ra2, vf * g1, f2)
    return joined, (wg, wf, q1, vg, vf, q2)


def unmerge(weights, va, vb):
    wg, wf, q1, vg, vf, q2 = weights
    inner_right = vg * va + vf * vb + q2
    inner_left = wg * va + wf * inner_right + q1
    return inner_left, inner_right


def solve_pair(ea, ra, eb, rb, g):
    s = 1.0 / (ea + g)
    w = g * s
    vb = (rb + w * ra) / (eb + w * ea)
    return w * vb + ra * s, vb


def merge_all(chains):
    levels = []
    while len(chains) > 1:
        pairs = [merge(chains[i], chains[i + 1]) for i in range(0, len(chains), 2)]
        chains = [p[0] for p in pairs]
        levels.append([p[1] for p in pairs])
    return chains[0], levels


def unmerge_all(levels, va, vb):
    ends = [(va, vb)]
    for level in reversed(levels):
        split = []
        for weights, (a, b) in zip(level, ends):
            inner_left, inner_right = unmerge(weights, a, b)
            split += [(a, inner_left), (inner_right, b)]
        ends = split
    return ends


def line_start(get_d, get_r, count):
    states = []
    for base in range(0, count, count // SEGMENTS):
        d0, d1 = get_d(base), get_d(base + 1)
        one = jnp.ones_like(d0)
        states.append((one, get_r(base), d0 + d1, one, get_r(base + 1), d1))
    return tuple(states)


def line_reduce(get_d, get_r, weights, count, first, last, states):
    size = count // SEGMENTS

    def body(i, states):
        new = []
        for k, (ea, ra, g, e, r, d) in enumerate(states):
            j = k * size + i
            d1 = get_d(j + 1)
            f = d + d1
            s = 1.0 / (e + g + f)
            wf, wg = f * s, g * s
            weights[0, j] = wf
            weights[1, j] = wg
            weights[2, j] = r * s
            new.append((ea + wg * e, ra + wg * r, wf * g, 1.0 + wf * e, get_r(j + 1) + wf * r, d1))
        return tuple(new)

    return lax.fori_loop(first, last, body, states)


def line_chain(get_d, states, count, edge):
    size = count // SEGMENTS
    chains = []
    for k, (ea, ra, g, e, r, d) in enumerate(states):
        f = d + get_d((k + 1) * size) if k + 1 < SEGMENTS else edge(d)
        chains.append((ea, ra, e, r, g, f))
    return merge_all(chains)


def line_back(put, weights, count, ends):
    size = count // SEGMENTS
    for k, (a, b) in enumerate(ends):
        put(k * size, a)
        put(k * size + size - 1, b)

    def body(t, values):
        new = []
        for k, v in enumerate(values):
            j = k * size + size - 2 - t
            v = weights[0, j] * v + (weights[1, j] * ends[k][0] + weights[2, j])
            put(j, v)
            new.append(v)
        return tuple(new)

    lax.fori_loop(0, size - 2, body, tuple(b for a, b in ends))


def kernel(ny, nz, rounds, vol, con, out, c_ref, t_ref, b_ref, d_ref, dt_ref, wx_ref, wy_ref, wz_ref, vx_ref, vy_ref,
           vz_ref, cur_ref, zr_ref, zi_ref, zsend, zbuf, zvsend, zv, ysend, yrecv,
           halo_s, halo_r, zs, zrs, zvs, zvr, ys, yr):
    depth, nx, cols = vol.shape
    rows = cols + 2 * PAD
    tall = depth + 2 * HALO
    chunks = cols // CHUNK
    ky = lax.axis_index("gy")
    kz = lax.axis_index("gz")

    def at(y, z):
        return {"gy": y, "gz": z}

    def exists(dy, dz):
        ok = True
        if dy:
            ok = (ky + dy >= 0) & (ky + dy < ny)
        if dz:
            ok = ok & (kz + dz >= 0) & (kz + dz < nz)
        return ok

    def partner(r):
        size = 2 ** r
        bit = lax.rem(lax.div(ky, size), 2)
        return bit, ky + size * (1 - 2 * bit)

    barrier = pltpu.get_barrier_semaphore()
    expected = jnp.int32(rounds)
    for dy, dz in DIRECTIONS:
        ok = exists(dy, dz)
        expected = expected + jnp.where(ok, 1, 0)

        @pl.when(ok)
        def _(dy=dy, dz=dz):
            pl.semaphore_signal(barrier, inc=1, device_id=at(ky + dy, kz + dz), device_id_type=MESH)

    for r in range(rounds):
        pl.semaphore_signal(barrier, inc=1, device_id=at(partner(r)[1], kz), device_id_type=MESH)
    @pl.loop(0, depth // 4)
    def _(k):
        for z in [4 * k, 4 * k + 1, 4 * k + 2, 4 * k + 3]:
            plane = vol[z]
            cur_ref[z, 0:nx, :] = plane
            c_ref[0, z + HALO, PAD:PAD + cols, :] = plane.T

    pl.semaphore_wait(barrier, expected)

    left = kz < nz // 2
    inward = jnp.where(left, 1, -1)
    order = jnp.where(left, kz, nz - 1 - kz)
    middle = order == nz // 2 - 1
    outermost = order == 0
    slot_out = jnp.where(middle, 1, 0)

    lane = lax.broadcasted_iota(jnp.int32, (STENCIL_ROWS, nx), 1)
    keep = {s: (lane >= s) if s > 0 else (lane < nx + s) for s in (-2, -1, 1, 2)}

    def shifted(value, s):
        return jnp.where(keep[s][:value.shape[0]], pltpu.roll(value, s % nx, 1), 0.0)

    contrast = con[...]
    squared = jnp.broadcast_to(contrast * contrast, (STENCIL_ROWS, nx))

    tall_x = nx + SKEW
    tall_y = cols + SKEW
    cur2 = cur_ref.reshape(depth * tall_x, cols)
    dt2 = dt_ref.reshape(depth * tall_x, cols)
    vx2 = vx_ref.reshape(depth * tall_x, cols)
    vy2 = vy_ref.reshape(depth * tall_y, nx)
    d2 = d_ref.reshape((depth + 2) * rows, nx)

    def finish(z, target):
        plane = (vx_ref[z, 0:nx, :] + (vy_ref[z, 0:cols, :] + vz_ref[z]).T) * (1.0 / 3.0)
        if target is None:
            out[z] = plane
        else:
            cur_ref[z, 0:nx, :] = plane
            target[z + HALO, PAD:PAD + cols, :] = plane.T

    def finish_edges(target):
        @pl.loop(0, HALO // 2)
        def _(k):
            for t in range(2):
                finish(2 * k + t, target)
                finish(depth - HALO + 2 * k + t, target)

    def finish_middle(target):
        @pl.loop(0, (depth - 2 * HALO) // 4)
        def _(k):
            for t in range(4):
                finish(HALO + 4 * k + t, target)

    parts = [(r0, min(STENCIL_ROWS, cols + 8 - r0)) for r0 in range(0, cols + 8, STENCIL_ROWS)]

    for step in range(STEPS):
        c4 = c_ref.at[step]
        c2 = c4.reshape(tall * rows, nx)

        def halo(i, c4=c4, step=step):
            dy, dz = DIRECTIONS[i]
            src_y = {0: (PAD, cols), 1: (cols, PAD), -1: (PAD, PAD)}[dy]
            dst_y = {0: (PAD, cols), 1: (0, PAD), -1: (PAD + cols, PAD)}[dy]
            src_z = {0: (HALO, depth), 1: (depth, HALO), -1: (HALO, HALO)}[dz]
            dst_z = {0: (HALO, depth), 1: (0, HALO), -1: (HALO + depth, HALO)}[dz]
            src = c4.at[pl.ds(*src_z), pl.ds(*src_y), :]
            dst = c4.at[pl.ds(*dst_z), pl.ds(*dst_y), :]
            copy = pltpu.make_async_remote_copy(
                src_ref=src, dst_ref=dst, send_sem=halo_s.at[step, i], recv_sem=halo_r.at[step, i],
                device_id=at(ky + dy, kz + dz), device_id_type=MESH)
            return copy, dst_z, dst_y

        def send(layers, halo=halo, c4=c4):
            for i, (dy, dz) in enumerate(DIRECTIONS):
                if (dz != 0) != layers:
                    continue
                copy, dst_z, dst_y = halo(i)

                @pl.when(exists(dy, dz))
                def _(copy=copy):
                    copy.start()

                @pl.when(jnp.logical_not(exists(-dy, -dz)))
                def _(dst_z=dst_z, dst_y=dst_y):
                    c4[pl.ds(*dst_z), pl.ds(*dst_y), :] = jnp.zeros((dst_z[1], dst_y[1], nx), jnp.float32)

        def receive(layers):
            for i, (dy, dz) in enumerate(DIRECTIONS):
                if (dz != 0) != layers:
                    continue
                copy = halo(i)[0]

                @pl.when(exists(-dy, -dz))
                def _(copy=copy):
                    copy.wait_recv()

        if step == 0:
            send(True)
        else:
            finish_edges(c4)
            send(True)
            finish_middle(c4)
        send(False)

        def blur_layers(z0, z1, pieces):
            @pl.loop(z0, z1)
            def _(z):
                for r0, size in pieces:
                    part = pl.ds(r0, size)
                    total = TAPS[2] * c4[z + 2, part, :]
                    total = total + TAPS[1] * (c4[z + 1, part, :] + c4[z + 3, part, :])
                    total = total + TAPS[0] * (c4[z, part, :] + c4[z + 4, part, :])
                    t_ref[z, pl.ds(r0, size), :] = total

        def blur(z0, z1):
            @pl.loop(z0, z1)
            def _(z):
                for r0, size in parts:
                    def tap(o):
                        return t_ref[z, pl.ds(r0 + 4 + o, size), :]
                    total = TAPS[2] * tap(0) + TAPS[1] * (tap(-1) + tap(1)) + TAPS[0] * (tap(-2) + tap(2))
                    b_ref[z, pl.ds(r0, size), :] = (
                        TAPS[2] * total + TAPS[1] * (shifted(total, 1) + shifted(total, -1))
                        + TAPS[0] * (shifted(total, 2) + shifted(total, -2)))

            @pl.when(ky == 0)
            def _():
                b_ref[z0:z1, PAD - 5:PAD - 4, :] = jnp.zeros((z1 - z0, 1, nx), jnp.float32)

            @pl.when(ky == ny - 1)
            def _():
                b_ref[z0:z1, cols + PAD - 4:cols + PAD - 3, :] = jnp.zeros((z1 - z0, 1, nx), jnp.float32)

        def diffuse(z0, z1):
            @pl.loop(z0, z1)
            def _(z):
                for r0, size in parts:
                    mid = b_ref[z + 1, pl.ds(r0 + 4, size), :]
                    grad_z = b_ref[z + 2, pl.ds(r0 + 4, size), :] - b_ref[z, pl.ds(r0 + 4, size), :]
                    grad_y = b_ref[z + 1, pl.ds(r0 + 5, size), :] - b_ref[z + 1, pl.ds(r0 + 3, size), :]
                    grad_x = shifted(mid, -1) - shifted(mid, 1)
                    square = (grad_x * grad_x + grad_y * grad_y + grad_z * grad_z) * 0.25
                    d_ref[z, pl.ds(r0 + PAD, size), :] = (SCALE * squared[:size]) / (squared[:size] + square)

        def turn(z0, z1):
            step_by = 2 if (z1 - z0) % 2 == 0 else 1

            @pl.loop(0, (z1 - z0) // step_by)
            def _(k):
                for t in range(step_by):
                    z = z0 + k * step_by + t
                    dt_ref[z, 0:nx, :] = d_ref[z + 1, PAD:PAD + cols, :].T

        own_rows = [(r0, min(STENCIL_ROWS, cols + PAD - r0)) for r0 in range(PAD, cols + PAD, STENCIL_ROWS)]
        halo_rows = [(0, PAD), (cols + PAD, PAD)]
        blur_layers(HALO, depth, own_rows)
        receive(False)
        blur_layers(HALO, depth, halo_rows)
        blur(HALO, depth)
        diffuse(HALO, depth - 2)
        turn(HALO - 1, depth - 3)
        receive(True)
        all_rows = own_rows + halo_rows
        blur_layers(0, HALO, all_rows)
        blur_layers(depth, depth + 4, all_rows)
        blur(0, HALO)
        blur(depth, depth + 4)

        @pl.when(kz == 0)
        def _():
            b_ref[1] = jnp.zeros(b_ref.shape[1:], jnp.float32)

        @pl.when(kz == nz - 1)
        def _():
            b_ref[depth + 2] = jnp.zeros(b_ref.shape[1:], jnp.float32)

        diffuse(0, HALO)
        diffuse(depth - 2, depth + 2)
        turn(0, HALO - 1)
        turn(depth - 3, depth)

        for i, (dy, dz) in enumerate(DIRECTIONS):
            copy = halo(i)[0]

            @pl.when(exists(dy, dz))
            def _(copy=copy):
                copy.wait_send()

        def z_copy(c, slot):
            return pltpu.make_async_remote_copy(
                src_ref=zsend.at[step, c], dst_ref=zbuf.at[step, slot, c], send_sem=zs.at[step, c],
                recv_sem=zrs.at[step, slot, c], device_id=at(ky, kz + inward), device_id_type=MESH)

        def z_back(c):
            return pltpu.make_async_remote_copy(
                src_ref=zvsend.at[step, c], dst_ref=zv.at[step, c], send_sem=zvs.at[step, c],
                recv_sem=zvr.at[step, c], device_id=at(ky, kz - inward), device_id_type=MESH)

        def z_inward(c, carry):
            own = pl.ds(pl.multiple_of(c * CHUNK, CHUNK), CHUNK)

            @pl.when(jnp.logical_not(outermost))
            def _():
                z_copy(c, 0).wait_recv()
                zr_ref[0, own, :] += zbuf[step, 0, c, 0]
                zr_ref[1, own, :] += zbuf[step, 0, c, 1]

            eo, ro, ei, ri, g, f = [zr_ref[j, own, :] for j in range(6)]
            s = 1.0 / (eo + g)
            w = g * s
            ei = ei + w * eo
            ri = ri + w * ro
            s2 = 1.0 / (ei + f)
            u = f * s2
            zi_ref[0, own, :] = w
            zi_ref[1, own, :] = ro * s
            zi_ref[2, own, :] = ei
            zi_ref[3, own, :] = ri
            zi_ref[4, own, :] = u
            zi_ref[5, own, :] = ri * s2
            zsend[step, c, 0] = u * ei
            zsend[step, c, 1] = u * ri
            z_copy(c, slot_out).start()
            return carry

        def z_outward(c, carry):
            own = pl.ds(pl.multiple_of(c * CHUNK, CHUNK), CHUNK)

            @pl.when(middle)
            def _():
                z_copy(c, 1).wait_recv()
                zr_ref[0, own, :] = (zi_ref[3, own, :] + zbuf[step, 1, c, 1]) / (zi_ref[2, own, :] + zbuf[step, 1, c, 0])

            @pl.when(jnp.logical_not(middle))
            def _():
                z_back(c).wait_recv()
                zr_ref[0, own, :] = zi_ref[4, own, :] * zv[step, c] + zi_ref[5, own, :]

            vi = zr_ref[0, own, :]
            vo = zi_ref[0, own, :] * vi + zi_ref[1, own, :]

            @pl.when(jnp.logical_not(outermost))
            def _():
                zvsend[step, c] = vo
                z_back(c).start()

            va = jnp.where(left, vo, vi)
            v = jnp.where(left, vi, vo)
            vz_ref[0, own, :] = va
            vz_ref[depth - 1, own, :] = v
            for i in range(depth - 2, 0, -1):
                v = wz_ref[0, i, own, :] * v + (wz_ref[1, i, own, :] * va + wz_ref[2, i, own, :])
                vz_ref[i, own, :] = v
            return carry

        @pl.loop(0, chunks)
        def _(c):
            y0 = pl.multiple_of(c * CHUNK, CHUNK)
            part = pl.ds(y0 + PAD, CHUNK)
            own = pl.ds(y0, CHUNK)
            d = d_ref[1, part, :]
            f_lo = jnp.where(kz > 0, d_ref[0, part, :] + d, 0.0)
            d_next = d_ref[2, part, :]
            g = d + d_next
            d = d_next
            ea = jnp.ones_like(g)
            ra = c4[HALO, part, :]
            e = ea
            r = c4[HALO + 1, part, :]
            for i in range(1, depth - 1):
                d_next = d_ref[i + 2, part, :]
                f = d + d_next
                d = d_next
                s = 1.0 / (e + g + f)
                wf, wg = f * s, g * s
                wz_ref[0, i, own, :] = wf
                wz_ref[1, i, own, :] = wg
                wz_ref[2, i, own, :] = r * s
                ea = ea + wg * e
                ra = ra + wg * r
                e = 1.0 + wf * e
                r = c4[HALO + i + 1, part, :] + wf * r
                g = wf * g
            f_hi = jnp.where(kz < nz - 1, d + d_ref[depth + 1, part, :], 0.0)
            zr_ref[0, own, :] = jnp.where(left, ea, e)
            zr_ref[1, own, :] = jnp.where(left, ra, r)
            zr_ref[2, own, :] = jnp.where(left, e, ea)
            zr_ref[3, own, :] = jnp.where(left, r, ra)
            zr_ref[4, own, :] = g
            zr_ref[5, own, :] = jnp.where(left, f_hi, f_lo)

            @pl.when(outermost)
            def _():
                z_inward(c, 0)


        def dx(i):
            return dt2[pl.ds(i, depth, stride=tall_x), :]

        def rx(i):
            return cur2[pl.ds(i, depth, stride=tall_x), :]

        def dy_(i):
            return d2[pl.ds(i + rows + PAD, depth, stride=rows), :]

        def ry(i):
            return c2[pl.ds(i + HALO * rows + PAD, depth, stride=rows), :]

        def put_x(i, v):
            vx2[pl.ds(i, depth, stride=tall_x), :] = v

        def put_y(i, v):
            vy2[pl.ds(i, depth, stride=tall_y), :] = v

        states = line_start(dy_, ry, cols)
        states = line_reduce(dy_, ry, wy_ref, cols, 1, cols // SEGMENTS - 1, states)
        chain, levels_y = line_chain(
            dy_, states, cols, lambda d: jnp.where(ky < ny - 1, d + dy_(cols), 0.0))

        def y_copy(r):
            return pltpu.make_async_remote_copy(
                src_ref=ysend.at[step, r], dst_ref=yrecv.at[step, r], send_sem=ys.at[step, r],
                recv_sem=yr.at[step, r], device_id=at(partner(r)[1], kz), device_id_type=MESH)

        def y_start(r, chain):
            for j in range(6):
                ysend[step, r, j] = chain[j]
            y_copy(r).start()

        if rounds:
            y_start(0, chain)

        size_x = nx // SEGMENTS
        cuts = [1 + (size_x - 2) * k // chunks for k in range(chunks + 1)]

        def x_piece(k, states):
            states = line_reduce(dx, rx, wx_ref, nx, cuts[k], cuts[k + 1], states)

            @pl.when(jnp.logical_not(outermost))
            def _():
                z_inward(k, 0)

            return states

        states = line_start(dx, rx, nx)
        for k in range(chunks // 2):
            states = x_piece(k, states)

        weights = []

        def y_round(r, chain):
            y_copy(r).wait_recv()
            other = tuple(yrecv[step, r, j] for j in range(6))
            first = partner(r)[0] == 0
            pair_l = tuple(jnp.where(first, a, b) for a, b in zip(chain, other))
            pair_r = tuple(jnp.where(first, b, a) for a, b in zip(chain, other))
            chain, w = merge(pair_l, pair_r)
            weights.append(w)
            if r + 1 < rounds:
                y_start(r + 1, chain)
            return chain

        if rounds > 0:
            chain = y_round(0, chain)
        for k in range(chunks // 2, chunks):
            states = x_piece(k, states)
        x_chain, levels_x = line_chain(dx, states, nx, jnp.zeros_like)
        if rounds > 1:
            chain = y_round(1, chain)
        line_back(put_x, wx_ref, nx, unmerge_all(levels_x, *solve_pair(*x_chain[:5])))

        @pl.when(jnp.logical_not(outermost))
        def _():
            lax.fori_loop(0, chunks, z_outward, 0)

        for r in range(2, rounds):
            chain = y_round(r, chain)

        va, vb = solve_pair(*chain[:5])
        for r in range(rounds - 1, -1, -1):
            first = partner(r)[0] == 0
            inner_l, inner_r = unmerge(weights[r], va, vb)
            va = jnp.where(first, va, inner_r)
            vb = jnp.where(first, inner_l, vb)
        line_back(put_y, wy_ref, cols, unmerge_all(levels_y, va, vb))

        @pl.when(outermost)
        def _():
            lax.fori_loop(0, chunks, z_outward, 0)

        for r in range(rounds):
            y_copy(r).wait_send()

        @pl.loop(0, chunks)
        def _(c):
            z_copy(c, slot_out).wait_send()

            @pl.when(jnp.logical_not(outermost))
            def _():
                z_back(c).wait_send()

    @pl.loop(0, depth // 4)
    def _(k):
        for t in range(4):
            finish(4 * k + t, None)


def on_device(volume, contrast):
    depth, nx, cols = volume.shape
    ny = lax.axis_size("gy")
    nz = lax.axis_size("gz")
    rounds = ny.bit_length() - 1
    assert 2 ** rounds == ny and nz % 2 == 0 and nz >= 2
    rows = cols + 2 * PAD
    chunks = cols // CHUNK
    f32 = jnp.float32
    dma = pltpu.SemaphoreType.DMA
    count = len(DIRECTIONS)
    return pl.pallas_call(
        functools.partial(kernel, ny, nz, rounds),
        out_shape=jax.ShapeDtypeStruct(volume.shape, f32),
        in_specs=[pl.BlockSpec(memory_space=pltpu.VMEM)] * 2,
        out_specs=pl.BlockSpec(memory_space=pltpu.VMEM),
        scratch_shapes=[
            pltpu.VMEM((STEPS, depth + 2 * HALO, rows, nx), f32),
            pltpu.VMEM((depth + 4, rows, nx), f32),
            pltpu.VMEM((depth + 4, rows + 16, nx), f32),
            pltpu.VMEM((depth + 2, rows, nx), f32),
            pltpu.VMEM((depth, nx + SKEW, cols), f32),
            pltpu.VMEM((3, nx, depth, cols), f32),
            pltpu.VMEM((3, cols, depth, nx), f32),
            pltpu.VMEM((3, depth, cols, nx), f32),
            pltpu.VMEM((depth, nx + SKEW, cols), f32),
            pltpu.VMEM((depth, cols + SKEW, nx), f32),
            pltpu.VMEM((depth, cols, nx), f32),
            pltpu.VMEM((depth, nx + SKEW, cols), f32),
            pltpu.VMEM((6, cols, nx), f32),
            pltpu.VMEM((6, cols, nx), f32),
            pltpu.VMEM((STEPS, chunks, 2, CHUNK, nx), f32),
            pltpu.VMEM((STEPS, 2, chunks, 2, CHUNK, nx), f32),
            pltpu.VMEM((STEPS, chunks, CHUNK, nx), f32),
            pltpu.VMEM((STEPS, chunks, CHUNK, nx), f32),
            pltpu.VMEM((STEPS, max(rounds, 1), 6, depth, nx), f32),
            pltpu.VMEM((STEPS, max(rounds, 1), 6, depth, nx), f32),
            dma((STEPS, count)), dma((STEPS, count)),
            dma((STEPS, chunks)), dma((STEPS, 2, chunks)),
            dma((STEPS, chunks)), dma((STEPS, chunks)),
            dma((STEPS, max(rounds, 1))), dma((STEPS, max(rounds, 1))),
        ],
        compiler_params=pltpu.CompilerParams(
            collective_id=0, has_side_effects=True, vmem_limit_bytes=48 * 2 ** 20
        ),
    )(volume, contrast.reshape(1, nx))


def solution(mesh):
    in_specs = (P("gz", None, "gy"), P())
    out_specs = P("gz", None, "gy")
    return jax.shard_map(
        on_device, mesh=mesh, in_specs=in_specs, out_specs=out_specs, check_vma=False
    )
```

```python
import functools

import jax
import jax.numpy as jnp
from jax import lax
from jax.experimental import pallas as pl
from jax.experimental.pallas import tpu as pltpu
from jax.sharding import PartitionSpec as P

STEPS = 2
TAPS = (0.05448868, 0.24420134, 0.40261995, 0.24420134, 0.05448868)
SCALE = 600.0
MESH = pl.DeviceIdType.MESH
DIRECTIONS = [(dy, dz) for dz in (-1, 1, 0) for dy in (0, -1, 1) if (dy, dz) != (0, 0)]
PAD = 8
HALO = 4
CHUNK = 32
STENCIL_ROWS = 48
SEGMENTS = 4
SKEW = 8


def merge(left, right):
    ea, ra, eb, rb, g, f = left
    ea2, ra2, eb2, rb2, g2, f2 = right
    s1 = 1.0 / (eb + g + f)
    wg, wf, q1 = g * s1, f * s1, rb * s1
    ea = ea + wg * eb
    ra = ra + wg * rb
    ea2 = ea2 + wf * eb
    ra2 = ra2 + wf * rb
    g1 = wf * g
    s2 = 1.0 / (ea2 + g1 + g2)
    vg, vf, q2 = g1 * s2, g2 * s2, ra2 * s2
    joined = (ea + vg * ea2, ra + vg * ra2, eb2 + vf * ea2, rb2 + vf * ra2, vf * g1, f2)
    return joined, (wg, wf, q1, vg, vf, q2)


def unmerge(weights, va, vb):
    wg, wf, q1, vg, vf, q2 = weights
    inner_right = vg * va + vf * vb + q2
    inner_left = wg * va + wf * inner_right + q1
    return inner_left, inner_right


def solve_pair(ea, ra, eb, rb, g):
    s = 1.0 / (ea + g)
    w = g * s
    vb = (rb + w * ra) / (eb + w * ea)
    return w * vb + ra * s, vb


def merge_all(chains):
    levels = []
    while len(chains) > 1:
        pairs = [merge(chains[i], chains[i + 1]) for i in range(0, len(chains), 2)]
        chains = [p[0] for p in pairs]
        levels.append([p[1] for p in pairs])
    return chains[0], levels


def unmerge_all(levels, va, vb):
    ends = [(va, vb)]
    for level in reversed(levels):
        split = []
        for weights, (a, b) in zip(level, ends):
            inner_left, inner_right = unmerge(weights, a, b)
            split += [(a, inner_left), (inner_right, b)]
        ends = split
    return ends


def line_start(get_d, get_r, count):
    states = []
    for base in range(0, count, count // SEGMENTS):
        d0, d1 = get_d(base), get_d(base + 1)
        one = jnp.ones_like(d0)
        states.append((one, get_r(base), d0 + d1, one, get_r(base + 1), d1))
    return tuple(states)


def line_reduce(get_d, get_r, weights, count, first, last, states):
    size = count // SEGMENTS

    def body(i, states):
        new = []
        for k, (ea, ra, g, e, r, d) in enumerate(states):
            j = k * size + i
            d1 = get_d(j + 1)
            f = d + d1
            s = 1.0 / (e + g + f)
            wf, wg = f * s, g * s
            weights[0, j] = wf
            weights[1, j] = wg
            weights[2, j] = r * s
            new.append((ea + wg * e, ra + wg * r, wf * g, 1.0 + wf * e, get_r(j + 1) + wf * r, d1))
        return tuple(new)

    return lax.fori_loop(first, last, body, states)


def line_chain(get_d, states, count, edge):
    size = count // SEGMENTS
    chains = []
    for k, (ea, ra, g, e, r, d) in enumerate(states):
        f = d + get_d((k + 1) * size) if k + 1 < SEGMENTS else edge(d)
        chains.append((ea, ra, e, r, g, f))
    return merge_all(chains)


def line_back(put, weights, count, ends):
    size = count // SEGMENTS
    for k, (a, b) in enumerate(ends):
        put(k * size, a)
        put(k * size + size - 1, b)

    def body(t, values):
        new = []
        for k, v in enumerate(values):
            j = k * size + size - 2 - t
            v = weights[0, j] * v + (weights[1, j] * ends[k][0] + weights[2, j])
            put(j, v)
            new.append(v)
        return tuple(new)

    lax.fori_loop(0, size - 2, body, tuple(b for a, b in ends), unroll=3)


def kernel(ny, nz, rounds, vol, con, out, c_ref, t_ref, b_ref, d_ref, dt_ref, wx_ref, wy_ref, wz_ref, vx_ref, vy_ref,
           vz_ref, cur_ref, zr_ref, zi_ref, zsend, zbuf, zvsend, zv, ysend, yrecv,
           halo_s, halo_r, zs, zrs, zvs, zvr, ys, yr):
    depth, nx, cols = vol.shape
    rows = cols + 2 * PAD
    tall = depth + 2 * HALO
    chunks = cols // CHUNK
    ky = lax.axis_index("gy")
    kz = lax.axis_index("gz")

    def at(y, z):
        return {"gy": y, "gz": z}

    def exists(dy, dz):
        ok = True
        if dy:
            ok = (ky + dy >= 0) & (ky + dy < ny)
        if dz:
            ok = ok & (kz + dz >= 0) & (kz + dz < nz)
        return ok

    def partner(r):
        size = 2 ** r
        bit = lax.rem(lax.div(ky, size), 2)
        return bit, ky + size * (1 - 2 * bit)

    barrier = pltpu.get_barrier_semaphore()
    expected = jnp.int32(rounds)
    for dy, dz in DIRECTIONS:
        ok = exists(dy, dz)
        expected = expected + jnp.where(ok, 1, 0)

        @pl.when(ok)
        def _(dy=dy, dz=dz):
            pl.semaphore_signal(barrier, inc=1, device_id=at(ky + dy, kz + dz), device_id_type=MESH)

    for r in range(rounds):
        pl.semaphore_signal(barrier, inc=1, device_id=at(partner(r)[1], kz), device_id_type=MESH)
    @pl.loop(0, depth // 4)
    def _(k):
        for z in [4 * k, 4 * k + 1, 4 * k + 2, 4 * k + 3]:
            plane = vol[z]
            cur_ref[z, 0:nx, :] = plane
            c_ref[0, z + HALO, PAD:PAD + cols, :] = plane.T

    pl.semaphore_wait(barrier, expected)

    left = kz < nz // 2
    inward = jnp.where(left, 1, -1)
    order = jnp.where(left, kz, nz - 1 - kz)
    middle = order == nz // 2 - 1
    outermost = order == 0
    slot_out = jnp.where(middle, 1, 0)

    lane = lax.broadcasted_iota(jnp.int32, (STENCIL_ROWS, nx), 1)
    keep = {s: (lane >= s) if s > 0 else (lane < nx + s) for s in (-2, -1, 1, 2)}

    def shifted(value, s):
        return jnp.where(keep[s][:value.shape[0]], pltpu.roll(value, s % nx, 1), 0.0)

    contrast = con[...]
    squared = jnp.broadcast_to(contrast * contrast, (STENCIL_ROWS, nx))

    tall_x = nx + SKEW
    tall_y = cols + SKEW
    cur2 = cur_ref.reshape(depth * tall_x, cols)
    dt2 = dt_ref.reshape(depth * tall_x, cols)
    vx2 = vx_ref.reshape(depth * tall_x, cols)
    vy2 = vy_ref.reshape(depth * tall_y, nx)
    d2 = d_ref.reshape((depth + 2) * rows, nx)

    def finish(z, target):
        plane = (vx_ref[z, 0:nx, :] + (vy_ref[z, 0:cols, :] + vz_ref[z]).T) * (1.0 / 3.0)
        if target is None:
            out[z] = plane
        else:
            cur_ref[z, 0:nx, :] = plane
            target[z + HALO, PAD:PAD + cols, :] = plane.T

    def finish_edges(target):
        @pl.loop(0, HALO // 2)
        def _(k):
            for t in range(2):
                finish(2 * k + t, target)
                finish(depth - HALO + 2 * k + t, target)

    def finish_middle(target):
        @pl.loop(0, (depth - 2 * HALO) // 4)
        def _(k):
            for t in range(4):
                finish(HALO + 4 * k + t, target)

    parts = [(r0, min(STENCIL_ROWS, cols + 8 - r0)) for r0 in range(0, cols + 8, STENCIL_ROWS)]

    for step in range(STEPS):
        c4 = c_ref.at[step]
        c2 = c4.reshape(tall * rows, nx)

        def halo(i, c4=c4, step=step):
            dy, dz = DIRECTIONS[i]
            src_y = {0: (PAD, cols), 1: (cols, PAD), -1: (PAD, PAD)}[dy]
            dst_y = {0: (PAD, cols), 1: (0, PAD), -1: (PAD + cols, PAD)}[dy]
            src_z = {0: (HALO, depth), 1: (depth, HALO), -1: (HALO, HALO)}[dz]
            dst_z = {0: (HALO, depth), 1: (0, HALO), -1: (HALO + depth, HALO)}[dz]
            src = c4.at[pl.ds(*src_z), pl.ds(*src_y), :]
            dst = c4.at[pl.ds(*dst_z), pl.ds(*dst_y), :]
            copy = pltpu.make_async_remote_copy(
                src_ref=src, dst_ref=dst, send_sem=halo_s.at[step, i], recv_sem=halo_r.at[step, i],
                device_id=at(ky + dy, kz + dz), device_id_type=MESH)
            return copy, dst_z, dst_y

        def send(layers, halo=halo, c4=c4):
            for i, (dy, dz) in enumerate(DIRECTIONS):
                if (dz != 0) != layers:
                    continue
                copy, dst_z, dst_y = halo(i)

                @pl.when(exists(dy, dz))
                def _(copy=copy):
                    copy.start()

                @pl.when(jnp.logical_not(exists(-dy, -dz)))
                def _(dst_z=dst_z, dst_y=dst_y):
                    c4[pl.ds(*dst_z), pl.ds(*dst_y), :] = jnp.zeros((dst_z[1], dst_y[1], nx), jnp.float32)

        def receive(layers):
            for i, (dy, dz) in enumerate(DIRECTIONS):
                if (dz != 0) != layers:
                    continue
                copy = halo(i)[0]

                @pl.when(exists(-dy, -dz))
                def _(copy=copy):
                    copy.wait_recv()

        if step == 0:
            send(True)
        else:
            finish_edges(c4)
            send(True)
            finish_middle(c4)
        send(False)

        def blur_layers(z0, z1, pieces):
            @pl.loop(z0, z1)
            def _(z):
                for r0, size in pieces:
                    part = pl.ds(r0, size)
                    total = TAPS[2] * c4[z + 2, part, :]
                    total = total + TAPS[1] * (c4[z + 1, part, :] + c4[z + 3, part, :])
                    total = total + TAPS[0] * (c4[z, part, :] + c4[z + 4, part, :])
                    t_ref[z, pl.ds(r0, size), :] = total

        def blur(z0, z1):
            @pl.loop(z0, z1, unroll=2)
            def _(z):
                for r0, size in parts:
                    def tap(o):
                        return t_ref[z, pl.ds(r0 + 4 + o, size), :]
                    total = TAPS[2] * tap(0) + TAPS[1] * (tap(-1) + tap(1)) + TAPS[0] * (tap(-2) + tap(2))
                    b_ref[z, pl.ds(r0, size), :] = (
                        TAPS[2] * total + TAPS[1] * (shifted(total, 1) + shifted(total, -1))
                        + TAPS[0] * (shifted(total, 2) + shifted(total, -2)))

            @pl.when(ky == 0)
            def _():
                b_ref[z0:z1, PAD - 5:PAD - 4, :] = jnp.zeros((z1 - z0, 1, nx), jnp.float32)

            @pl.when(ky == ny - 1)
            def _():
                b_ref[z0:z1, cols + PAD - 4:cols + PAD - 3, :] = jnp.zeros((z1 - z0, 1, nx), jnp.float32)

        def diffuse(z0, z1):
            @pl.loop(z0, z1, unroll=2)
            def _(z):
                for r0, size in parts:
                    mid = b_ref[z + 1, pl.ds(r0 + 4, size), :]
                    grad_z = b_ref[z + 2, pl.ds(r0 + 4, size), :] - b_ref[z, pl.ds(r0 + 4, size), :]
                    grad_y = b_ref[z + 1, pl.ds(r0 + 5, size), :] - b_ref[z + 1, pl.ds(r0 + 3, size), :]
                    grad_x = shifted(mid, -1) - shifted(mid, 1)
                    square = (grad_x * grad_x + grad_y * grad_y + grad_z * grad_z) * 0.25
                    d_ref[z, pl.ds(r0 + PAD, size), :] = (SCALE * squared[:size]) / (squared[:size] + square)

        def turn(z0, z1):
            step_by = 2 if (z1 - z0) % 2 == 0 else 1

            @pl.loop(0, (z1 - z0) // step_by)
            def _(k):
                for t in range(step_by):
                    z = z0 + k * step_by + t
                    dt_ref[z, 0:nx, :] = d_ref[z + 1, PAD:PAD + cols, :].T

        own_rows = [(r0, min(STENCIL_ROWS, cols + PAD - r0)) for r0 in range(PAD, cols + PAD, STENCIL_ROWS)]
        halo_rows = [(0, PAD), (cols + PAD, PAD)]
        blur_layers(HALO, depth, own_rows)
        receive(False)
        blur_layers(HALO, depth, halo_rows)
        blur(HALO, depth)
        diffuse(HALO, depth - 2)
        turn(HALO - 1, depth - 3)
        receive(True)
        all_rows = own_rows + halo_rows
        blur_layers(0, HALO, all_rows)
        blur_layers(depth, depth + 4, all_rows)
        blur(0, HALO)
        blur(depth, depth + 4)

        @pl.when(kz == 0)
        def _():
            b_ref[1] = jnp.zeros(b_ref.shape[1:], jnp.float32)

        @pl.when(kz == nz - 1)
        def _():
            b_ref[depth + 2] = jnp.zeros(b_ref.shape[1:], jnp.float32)

        diffuse(0, HALO)
        diffuse(depth - 2, depth + 2)
        turn(0, HALO - 1)
        turn(depth - 3, depth)

        for i, (dy, dz) in enumerate(DIRECTIONS):
            copy = halo(i)[0]

            @pl.when(exists(dy, dz))
            def _(copy=copy):
                copy.wait_send()

        def z_copy(c, slot):
            return pltpu.make_async_remote_copy(
                src_ref=zsend.at[step, c], dst_ref=zbuf.at[step, slot, c], send_sem=zs.at[step, c],
                recv_sem=zrs.at[step, slot, c], device_id=at(ky, kz + inward), device_id_type=MESH)

        def z_back(c):
            return pltpu.make_async_remote_copy(
                src_ref=zvsend.at[step, c], dst_ref=zv.at[step, c], send_sem=zvs.at[step, c],
                recv_sem=zvr.at[step, c], device_id=at(ky, kz - inward), device_id_type=MESH)

        def z_inward(c, carry):
            own = pl.ds(pl.multiple_of(c * CHUNK, CHUNK), CHUNK)

            @pl.when(jnp.logical_not(outermost))
            def _():
                z_copy(c, 0).wait_recv()
                zr_ref[0, own, :] += zbuf[step, 0, c, 0]
                zr_ref[1, own, :] += zbuf[step, 0, c, 1]

            eo, ro, ei, ri, g, f = [zr_ref[j, own, :] for j in range(6)]
            s = 1.0 / (eo + g)
            w = g * s
            ei = ei + w * eo
            ri = ri + w * ro
            s2 = 1.0 / (ei + f)
            u = f * s2
            zi_ref[0, own, :] = w
            zi_ref[1, own, :] = ro * s
            zi_ref[2, own, :] = ei
            zi_ref[3, own, :] = ri
            zi_ref[4, own, :] = u
            zi_ref[5, own, :] = ri * s2
            zsend[step, c, 0] = u * ei
            zsend[step, c, 1] = u * ri
            z_copy(c, slot_out).start()
            return carry

        def z_outward(c, carry):
            own = pl.ds(pl.multiple_of(c * CHUNK, CHUNK), CHUNK)

            @pl.when(middle)
            def _():
                z_copy(c, 1).wait_recv()
                zr_ref[0, own, :] = (zi_ref[3, own, :] + zbuf[step, 1, c, 1]) / (zi_ref[2, own, :] + zbuf[step, 1, c, 0])

            @pl.when(jnp.logical_not(middle))
            def _():
                z_back(c).wait_recv()
                zr_ref[0, own, :] = zi_ref[4, own, :] * zv[step, c] + zi_ref[5, own, :]

            vi = zr_ref[0, own, :]
            vo = zi_ref[0, own, :] * vi + zi_ref[1, own, :]

            @pl.when(jnp.logical_not(outermost))
            def _():
                zvsend[step, c] = vo
                z_back(c).start()

            va = jnp.where(left, vo, vi)
            v = jnp.where(left, vi, vo)
            vz_ref[0, own, :] = va
            vz_ref[depth - 1, own, :] = v
            for i in range(depth - 2, 0, -1):
                v = wz_ref[0, i, own, :] * v + (wz_ref[1, i, own, :] * va + wz_ref[2, i, own, :])
                vz_ref[i, own, :] = v
            return carry

        @pl.loop(0, chunks)
        def _(c):
            y0 = pl.multiple_of(c * CHUNK, CHUNK)
            part = pl.ds(y0 + PAD, CHUNK)
            own = pl.ds(y0, CHUNK)
            d = d_ref[1, part, :]
            f_lo = jnp.where(kz > 0, d_ref[0, part, :] + d, 0.0)
            d_next = d_ref[2, part, :]
            g = d + d_next
            d = d_next
            ea = jnp.ones_like(g)
            ra = c4[HALO, part, :]
            e = ea
            r = c4[HALO + 1, part, :]
            for i in range(1, depth - 1):
                d_next = d_ref[i + 2, part, :]
                f = d + d_next
                d = d_next
                s = 1.0 / (e + g + f)
                wf, wg = f * s, g * s
                wz_ref[0, i, own, :] = wf
                wz_ref[1, i, own, :] = wg
                wz_ref[2, i, own, :] = r * s
                ea = ea + wg * e
                ra = ra + wg * r
                e = 1.0 + wf * e
                r = c4[HALO + i + 1, part, :] + wf * r
                g = wf * g
            f_hi = jnp.where(kz < nz - 1, d + d_ref[depth + 1, part, :], 0.0)
            zr_ref[0, own, :] = jnp.where(left, ea, e)
            zr_ref[1, own, :] = jnp.where(left, ra, r)
            zr_ref[2, own, :] = jnp.where(left, e, ea)
            zr_ref[3, own, :] = jnp.where(left, r, ra)
            zr_ref[4, own, :] = g
            zr_ref[5, own, :] = jnp.where(left, f_hi, f_lo)

            @pl.when(outermost)
            def _():
                z_inward(c, 0)


        def dx(i):
            return dt2[pl.ds(i, depth, stride=tall_x), :]

        def rx(i):
            return cur2[pl.ds(i, depth, stride=tall_x), :]

        def dy_(i):
            return d2[pl.ds(i + rows + PAD, depth, stride=rows), :]

        def ry(i):
            return c2[pl.ds(i + HALO * rows + PAD, depth, stride=rows), :]

        def put_x(i, v):
            vx2[pl.ds(i, depth, stride=tall_x), :] = v

        def put_y(i, v):
            vy2[pl.ds(i, depth, stride=tall_y), :] = v

        states = line_start(dy_, ry, cols)
        states = line_reduce(dy_, ry, wy_ref, cols, 1, cols // SEGMENTS - 1, states)
        chain, levels_y = line_chain(
            dy_, states, cols, lambda d: jnp.where(ky < ny - 1, d + dy_(cols), 0.0))

        def y_copy(r):
            return pltpu.make_async_remote_copy(
                src_ref=ysend.at[step, r], dst_ref=yrecv.at[step, r], send_sem=ys.at[step, r],
                recv_sem=yr.at[step, r], device_id=at(partner(r)[1], kz), device_id_type=MESH)

        def y_start(r, chain):
            for j in range(6):
                ysend[step, r, j] = chain[j]
            y_copy(r).start()

        if rounds:
            y_start(0, chain)

        size_x = nx // SEGMENTS
        cuts = [1 + (size_x - 2) * k // chunks for k in range(chunks + 1)]

        def x_piece(k, states):
            states = line_reduce(dx, rx, wx_ref, nx, cuts[k], cuts[k + 1], states)

            @pl.when(jnp.logical_not(outermost))
            def _():
                z_inward(k, 0)

            return states

        states = line_start(dx, rx, nx)
        for k in range(chunks // 2):
            states = x_piece(k, states)

        weights = []

        def y_round(r, chain):
            y_copy(r).wait_recv()
            other = tuple(yrecv[step, r, j] for j in range(6))
            first = partner(r)[0] == 0
            pair_l = tuple(jnp.where(first, a, b) for a, b in zip(chain, other))
            pair_r = tuple(jnp.where(first, b, a) for a, b in zip(chain, other))
            chain, w = merge(pair_l, pair_r)
            weights.append(w)
            if r + 1 < rounds:
                y_start(r + 1, chain)
            return chain

        if rounds > 0:
            chain = y_round(0, chain)
        for k in range(chunks // 2, chunks):
            states = x_piece(k, states)
        x_chain, levels_x = line_chain(dx, states, nx, jnp.zeros_like)
        if rounds > 1:
            chain = y_round(1, chain)
        line_back(put_x, wx_ref, nx, unmerge_all(levels_x, *solve_pair(*x_chain[:5])))

        @pl.when(jnp.logical_not(outermost))
        def _():
            lax.fori_loop(0, chunks, z_outward, 0)

        for r in range(2, rounds):
            chain = y_round(r, chain)

        va, vb = solve_pair(*chain[:5])
        for r in range(rounds - 1, -1, -1):
            first = partner(r)[0] == 0
            inner_l, inner_r = unmerge(weights[r], va, vb)
            va = jnp.where(first, va, inner_r)
            vb = jnp.where(first, inner_l, vb)
        line_back(put_y, wy_ref, cols, unmerge_all(levels_y, va, vb))

        @pl.when(outermost)
        def _():
            lax.fori_loop(0, chunks, z_outward, 0)

        for r in range(rounds):
            y_copy(r).wait_send()

        @pl.loop(0, chunks)
        def _(c):
            z_copy(c, slot_out).wait_send()

            @pl.when(jnp.logical_not(outermost))
            def _():
                z_back(c).wait_send()

    @pl.loop(0, depth // 4)
    def _(k):
        for t in range(4):
            finish(4 * k + t, None)


def on_device(volume, contrast):
    depth, nx, cols = volume.shape
    ny = lax.axis_size("gy")
    nz = lax.axis_size("gz")
    rounds = ny.bit_length() - 1
    assert 2 ** rounds == ny and nz % 2 == 0 and nz >= 2
    rows = cols + 2 * PAD
    chunks = cols // CHUNK
    f32 = jnp.float32
    dma = pltpu.SemaphoreType.DMA
    count = len(DIRECTIONS)
    return pl.pallas_call(
        functools.partial(kernel, ny, nz, rounds),
        out_shape=jax.ShapeDtypeStruct(volume.shape, f32),
        in_specs=[pl.BlockSpec(memory_space=pltpu.VMEM)] * 2,
        out_specs=pl.BlockSpec(memory_space=pltpu.VMEM),
        scratch_shapes=[
            pltpu.VMEM((STEPS, depth + 2 * HALO, rows, nx), f32),
            pltpu.VMEM((depth + 4, rows, nx), f32),
            pltpu.VMEM((depth + 4, rows + 16, nx), f32),
            pltpu.VMEM((depth + 2, rows, nx), f32),
            pltpu.VMEM((depth, nx + SKEW, cols), f32),
            pltpu.VMEM((3, nx, depth, cols), f32),
            pltpu.VMEM((3, cols, depth, nx), f32),
            pltpu.VMEM((3, depth, cols, nx), f32),
            pltpu.VMEM((depth, nx + SKEW, cols), f32),
            pltpu.VMEM((depth, cols + SKEW, nx), f32),
            pltpu.VMEM((depth, cols, nx), f32),
            pltpu.VMEM((depth, nx + SKEW, cols), f32),
            pltpu.VMEM((6, cols, nx), f32),
            pltpu.VMEM((6, cols, nx), f32),
            pltpu.VMEM((STEPS, chunks, 2, CHUNK, nx), f32),
            pltpu.VMEM((STEPS, 2, chunks, 2, CHUNK, nx), f32),
            pltpu.VMEM((STEPS, chunks, CHUNK, nx), f32),
            pltpu.VMEM((STEPS, chunks, CHUNK, nx), f32),
            pltpu.VMEM((STEPS, max(rounds, 1), 6, depth, nx), f32),
            pltpu.VMEM((STEPS, max(rounds, 1), 6, depth, nx), f32),
            dma((STEPS, count)), dma((STEPS, count)),
            dma((STEPS, chunks)), dma((STEPS, 2, chunks)),
            dma((STEPS, chunks)), dma((STEPS, chunks)),
            dma((STEPS, max(rounds, 1))), dma((STEPS, max(rounds, 1))),
        ],
        compiler_params=pltpu.CompilerParams(
            collective_id=0, has_side_effects=True, vmem_limit_bytes=48 * 2 ** 20
        ),
    )(volume, contrast.reshape(1, nx))


def solution(mesh):
    in_specs = (P("gz", None, "gy"), P())
    out_specs = P("gz", None, "gy")
    return jax.shard_map(
        on_device, mesh=mesh, in_specs=in_specs, out_specs=out_specs, check_vma=False
    )
```
